256 devices in a mesh: band: 4 (over x), tile: 64 (over y, z, core).
Axes of the slice: x: 4, y: 4, z: 8, core: 2. Of those that a mesh axis runs over, the one named last changes fastest.
Arguments:
- granules: bfloat16 [1024, 16, 4096], P('tile', 'band'), may hold values from -6 to 6
- valid_rows: int32 [1024, 64], P('tile'), may hold values 0 or 1
- scene_order: int32 [1024], P('tile'), may hold values from 0 to 1023, each once
- intersections: int32 [1024, 4], P('tile'), may hold values from 0 to 63, all different within a row; in each aligned block of 16 rows (0 to 15, 16 to 31, ...) at most 2 rows name the same one
- row_resample: bfloat16 [1024, 4, 4096], P('tile'), may hold values from 0 to 1.4, as said below
- col_resample: bfloat16 [1024, 4, 4096], P('tile'), may hold values from 0 to 1.4, as said below
- w_in: bfloat16 [16, 256], replicated, may hold values from -1.5 to 1.5
- w_hidden: bfloat16 [2, 256, 256], replicated, may hold values from -0.375 to 0.375
- w_out: bfloat16 [256], replicated, may hold values from -1.5 to 1.5
Outputs:
- composite: float32 [16, 262144], P('band', 'tile')
The draws below stay inside these ranges and needn't reach their ends.
Inputs may be any that keep to these rules, and one draw needn't show every extreme that they name: `intersections`: each scene names 4 different output tiles; the 16 scenes of one device name any one tile at most 2 times, a bound that some block reaches. `scene_order`: each order number appears once. `row_resample`: nonnegative resampling weights. `col_resample`: nonnegative resampling weights.
All inputs are finite; a program needn't handle non-finite values. No bound on the sum of `valid_rows` on one device may be relied on, other than what follows from the above.
Results may differ from the reference program's by a relative error of at most 0.0031.
Values may be sent and summed in bfloat16 or wider, within the bound.
No kernel may reach another device: no remote copies, remote signals or barrier semaphores. Data moves between devices by JAX's collectives and lax.ppermute only.
A program may use at most 128 MiB of HBM per device.

```python
import math
import jax
import jax.numpy as jnp
import numpy as np
from jax import lax

BANDS = 16
HID = 256
LAYERS = 2
SIDE = 64
PIX = 4096
SC_DEV = 16
K = 4
HUBER_ITERS = 4
SMOOTH = 2
SCENES = 1024
CAP = 2
N_TILE = 64


def resample_matrix(key):
    positions = jnp.arange(SIDE)
    distance = jnp.abs(positions[:, None] - positions[None, :]).astype(jnp.float32)
    on_diagonal = (distance < 0.5).astype(jnp.float32)
    key_diag = jax.random.fold_in(key, 3)
    key_off = jax.random.fold_in(key, 5)
    diag_spread = jax.random.uniform(key_diag, (SCENES, K, SIDE, SIDE), jnp.float32, 0.6, 1.0)
    off_spread = jax.random.uniform(key_off, (SCENES, K, SIDE, SIDE), jnp.float32, 0.5, 1.5)
    dense_scale = 0.5 * SIDE ** (-0.5)
    background = dense_scale * off_spread * jnp.exp(-distance / (0.5 * SIDE))
    matrix = diag_spread * on_diagonal + background
    return matrix.reshape(SCENES, K, SIDE * SIDE).astype(jnp.bfloat16)


def draw_row_resample(key, part):
    return resample_matrix(jax.random.fold_in(key, 11))


def draw_col_resample(key, part):
    return resample_matrix(jax.random.fold_in(key, 23))


def plant(array, rng, least, top_value):
    shape = array.shape
    place = [jax.random.randint(jax.random.fold_in(rng, axis), (), 0, shape[axis]) for axis in range(len(shape))]
    array = array.at[tuple(place)].set(least)
    longest = shape.index(max(shape))
    place[longest] = (place[longest] + 1) % shape[longest]
    return array.at[tuple(place)].set(top_value)


def steps_of(key, dims, shards, least, largest):
    factor_of, own = 1.0, jax.random.fold_in(key, 6)
    for position, parts in shards:
        heights = jnp.exp(jax.random.uniform(jax.random.fold_in(own, position), (parts,), jnp.float32, least / len(shards), largest / len(shards)))
        factor_of = factor_of * jnp.repeat(heights, dims[position] // parts).reshape([-1 if axis == position else 1 for axis in range(len(dims))])
    return factor_of


def assign_block(key, own, number, rows, number_of, top, most, skew):
    sequence = jax.random.permutation(key, number_of)
    crowded, usual = portions_of(number_of, rows * top, most, skew, True), portions_of(number_of, rows * top, most, skew, False)
    places = jnp.arange(number_of)

    def named(tallies, turn):
        used = int((tallies > 0).sum())
        fixed = max(1, used // 4)
        shifted = fixed + (places - fixed + turn * (used - fixed)) % max(1, number_of - fixed)
        return jnp.zeros((number_of,), jnp.int32).at[sequence[jnp.where(places < fixed, places, shifted)]].set(jnp.asarray(tallies, jnp.int32))

    tallies = jnp.where(number % 4 == 0, named(crowded, number // 4), named(usual, number - number // 4 - 1))
    mixed = jax.random.permutation(jax.random.fold_in(own, 3), number_of)
    source_of, sink = mixed[0:number_of // 2 * 2:2], mixed[1:number_of // 2 * 2:2]
    margin = jnp.minimum(tallies[source_of] - 1, most - tallies[sink]) // 2
    margin = jnp.where((source_of == sequence[0]) | (sink == sequence[0]) | (tallies[sink] == 0), 0, jnp.maximum(margin, 0))
    shifted = jax.random.randint(jax.random.fold_in(own, 4), (number_of // 2,), 0, 1 << 20) % (margin + 1)
    tallies = tallies.at[source_of].add(-shifted).at[sink].add(shifted)
    items = jnp.searchsorted(jnp.cumsum(tallies), jnp.arange(rows * top), side="right").astype(jnp.int32)
    table = items.reshape(top, rows).T
    table = table[jax.random.permutation(jax.random.fold_in(own, 1), rows)]
    turn = jax.random.randint(jax.random.fold_in(own, 2), (rows, 1), 0, top)
    return jnp.take_along_axis(table, (jnp.arange(top)[None, :] + turn) % top, axis=1)


def portions_of(count, total, limit, lean, full):
    portions = [(1 << 20) // math.isqrt(standing ** lean) + 1 for standing in range(1, count + 1)]
    largest = limit if full else min(limit, max(-(-total // count), total * portions[0] // sum(portions)))
    least = 1 if total - largest >= count - 1 else 0
    holding, spare = [largest] + [least] * (count - 1), total - largest - least * (count - 1)
    while spare > 0:
        free = [i for i in range(1, count) if holding[i] < largest] or [i for i in range(1, count) if holding[i] < limit]
        whole, left = sum([portions[i] for i in free]), spare
        for i in free:
            extra = min(limit - holding[i], max(1, left * portions[i] // whole), spare)
            holding[i] = holding[i] + extra
            spare = spare - extra
    return np.array(holding)


def centred(rng, shape, scale, reach, pieces=(), kind=jnp.bfloat16):
    values = jax.random.normal(rng, shape, jnp.float32) * scale
    if len(pieces) > 0:
        values = steps_of(rng, shape, pieces, -0.22, 0.18) * values
    return jnp.clip(values, min=-reach, max=reach).astype(kind)


def setup_inputs(seed: int = 0) -> dict:
    arg_keys = jax.random.split(jax.random.key(seed), 10)
    granules = centred(arg_keys[0], (SCENES, BANDS, PIX), 1.0, 6.0, ((0, 64), (1, 4)))
    valid_rows = plant((jax.random.randint(arg_keys[1], (SCENES, SIDE), 0, 4) < 3).astype(jnp.int32), jax.random.fold_in(arg_keys[1], 1), 0, 1)
    scene_order = jax.random.permutation(arg_keys[2], SCENES).astype(jnp.int32)
    intersections_keys = jax.random.split(jax.random.fold_in(arg_keys[3], 1), SCENES // SC_DEV)
    intersections_turns = jax.random.permutation(jax.random.fold_in(arg_keys[3], 3), SCENES // SC_DEV)
    intersections = jax.vmap(lambda own, number: assign_block(jax.random.fold_in(arg_keys[3], 2), own, number, SC_DEV, N_TILE, K, CAP, 2))(intersections_keys, intersections_turns).reshape((SCENES, K))
    row_resample = draw_row_resample(jax.random.fold_in(arg_keys[9], 71), 0)
    col_resample = draw_col_resample(jax.random.fold_in(arg_keys[9], 71), 0)
    w_in = centred(arg_keys[6], (BANDS, HID), BANDS ** -0.5, 1.5)
    w_hidden = centred(arg_keys[7], (LAYERS, HID, HID), HID ** -0.5, 0.375)
    w_out = centred(arg_keys[8], (HID,), 0.25, 1.5)
    return dict(granules=granules, valid_rows=valid_rows, scene_order=scene_order, intersections=intersections, row_resample=row_resample, col_resample=col_resample, w_in=w_in, w_hidden=w_hidden, w_out=w_out)


prior_weight = 0.25
huber_delta = 0.5
edge_scale = 1.0
smooth_rate = 0.2


def cloud_weight(pixels, valid_pix, recency, w_in, w_hidden, w_out):
    hidden = jax.nn.silu(jnp.dot(pixels.T, w_in, preferred_element_type=jnp.float32)).astype(jnp.bfloat16)
    for repeat in range(LAYERS):
        hidden = jax.nn.silu(jnp.dot(hidden, w_hidden[repeat], preferred_element_type=jnp.float32)).astype(jnp.bfloat16)
    logits = jnp.dot(hidden, w_out, preferred_element_type=jnp.float32)
    return (jax.nn.sigmoid(-logits) * valid_pix * recency).astype(jnp.bfloat16)


def reproject(planes, rows_matrix, cols_matrix):
    half_done = jnp.einsum('ncil,njl->ncij', planes.astype(jnp.float32), cols_matrix.astype(jnp.float32)).astype(jnp.bfloat16)
    return jnp.einsum('nij,ncjl->ncil', rows_matrix.astype(jnp.float32), half_done.astype(jnp.float32)).astype(jnp.bfloat16)


def huber_merge(observed, weights):
    values = observed.astype(jnp.float32)
    plain = weights.astype(jnp.float32)[:, None, :]
    estimate = jnp.sum(plain * values, 0) / (jnp.sum(plain, 0) + prior_weight)
    for repeat in range(HUBER_ITERS):
        residual = values - estimate[None]
        huber_w = plain * huber_delta / jnp.maximum(jnp.abs(residual), huber_delta)
        estimate = jnp.sum(huber_w * values, 0) / (jnp.sum(huber_w, 0) + prior_weight)
    return estimate


def smooth_step(extended, first_col, total_cols):
    positions = first_col + jnp.arange(extended.shape[2] - 1)
    inside = ((positions >= 0) & (positions + 1 < total_cols)).astype(jnp.float32)
    across = extended[:, :, 1:] - extended[:, :, :-1]
    sideways = across / (1.0 + (across / edge_scale) ** 2) * inside
    centre = extended[:, :, 1:-1]
    upward_diff = centre[:, 1:, :] - centre[:, :-1, :]
    upward = upward_diff / (1.0 + (upward_diff / edge_scale) ** 2)
    zeros_row = jnp.zeros_like(upward[:, :1, :])
    vertical = jnp.concatenate([upward, zeros_row], 1) - jnp.concatenate([zeros_row, upward], 1)
    return centre + smooth_rate * (sideways[:, :, 1:] - sideways[:, :, :-1] + vertical)


def reference(granules, valid_rows, scene_order, intersections, row_resample, col_resample, w_in, w_hidden, w_out):
    recency = jnp.exp(1.4 * scene_order.astype(jnp.float32) / SCENES - 0.7)

    def one_scene(scene):
        valid_pix = jnp.repeat(valid_rows[scene].astype(jnp.float32), SIDE)
        return cloud_weight(granules[scene], valid_pix, recency[scene], w_in, w_hidden, w_out)

    weights = lax.map(one_scene, jnp.arange(SCENES).astype(jnp.int32))
    planes = jnp.concatenate([granules, weights[:, None, :]], 1)
    flat_dest = intersections.reshape(SCENES * K)
    entry_count = SCENES * K
    slot_count = N_TILE * CAP

    def one_owner(owner):
        sort_key = jnp.where(flat_dest == owner, jnp.arange(entry_count).astype(jnp.int32), entry_count).astype(jnp.int32)
        chosen = jnp.argsort(sort_key)[:slot_count].astype(jnp.int32)
        present = (sort_key[chosen] < entry_count).astype(jnp.bfloat16)
        scene_of = chosen // K
        which_k = chosen % K
        taken = planes[scene_of].reshape(slot_count, BANDS + 1, SIDE, SIDE)
        rows_taken = row_resample[scene_of, which_k].reshape(slot_count, SIDE, SIDE)
        cols_taken = col_resample[scene_of, which_k].reshape(slot_count, SIDE, SIDE)
        moved = reproject(taken, rows_taken, cols_taken)
        moved = moved.reshape(slot_count, BANDS + 1, PIX)
        return huber_merge(moved[:, :BANDS], moved[:, BANDS] * present[:, None])

    estimates = lax.map(one_owner, jnp.arange(N_TILE).astype(jnp.int32))
    field = estimates.reshape(N_TILE, BANDS, SIDE, SIDE).transpose(1, 2, 0, 3).reshape(BANDS, SIDE, N_TILE * SIDE)
    for repeat in range(SMOOTH):
        extended = jnp.pad(field, ((0, 0), (0, 0), (1, 1)))
        field = smooth_step(extended, -1, N_TILE * SIDE)
    return field.reshape(BANDS, SIDE, N_TILE, SIDE).transpose(0, 2, 1, 3).reshape(BANDS, N_TILE * PIX)
```

```python
import jax
import jax.numpy as jnp
import numpy as np
from jax import lax
from jax.experimental import pallas as pl
from jax.experimental.pallas import tpu as pltpu
from jax.sharding import PartitionSpec as P

HUBER_ITERS = 4
SMOOTH = 2

prior_weight = 0.25
huber_delta = 0.5
smooth_rate = 0.2

F32 = jnp.float32
BF16 = jnp.bfloat16
SIDE = 64


def dot(a, b, contract=((1,), (0,))):
    return lax.dot_general(a, b, (contract, ((), ())), preferred_element_type=F32)


def spread_matrix(count):
    out = np.zeros((count * SIDE, count * SIDE // 2), np.float32)
    for a in range(count):
        for i in range(SIDE):
            out[a * SIDE + i, count * (i // 2) + a] = 1.0
    return out


def parity_mask(rows):
    row = lax.broadcasted_iota(jnp.int32, (rows, 128), 0)
    lane = lax.broadcasted_iota(jnp.int32, (rows, 128), 1)
    return (row & 1) == (lane >> 6)


def spread_pair(both, mask):
    col = jnp.where(mask, both[:, :128], 0.0)
    col = (col + pltpu.roll(col, 64, 1)).astype(BF16)
    row = jnp.where(mask, both[:, 128:], 0.0).astype(BF16)
    return col, row


def reproject_kernel(x_ref, col_ref, row_ref, spread_ref, out_ref, scratch):
    mask = parity_mask(256)
    spread = spread_ref[...]
    for s in range(4):
        x = dot(spread, x_ref[s])
        x = jnp.where(mask, x, 0.0).astype(BF16)
        both = dot(spread, jnp.concatenate([col_ref[s], row_ref[s]], 1))
        col, row = spread_pair(both, mask)
        half = dot(x, col, ((1,), (1,)))
        for k in range(4):
            lanes = slice(k * SIDE, (k + 1) * SIDE)
            part = jnp.concatenate([half[c * SIDE : (c + 1) * SIDE, lanes] for c in range(4)], 1)
            part = part.astype(BF16)
            part = jnp.concatenate([part, part], 0)
            moved = dot(row[k * SIDE : (k + 1) * SIDE], part)
            for v in range(2):
                scratch[v, pl.ds(4 * s + k, SIDE, stride=16), :] = moved[:, v * 128 : (v + 1) * 128]
    for v in range(2):
        out_ref[:, :, v * 128 : (v + 1) * 128] = scratch[v].reshape(SIDE, 16, 128).astype(BF16)


def weight_kernel(w_ref, col_ref, row_ref, spread_ref, spread1_ref, out_ref, scratch):
    step = pl.program_id(0)
    mask = parity_mask(256)
    mask1 = parity_mask(SIDE)
    spread = spread_ref[...]
    spread1 = spread1_ref[...]
    for s in range(4):
        w = dot(spread1, w_ref[s])
        w = jnp.where(mask1, w, 0.0).astype(BF16)
        both = dot(spread, jnp.concatenate([col_ref[s], row_ref[s]], 1))
        col, row = spread_pair(both, mask)
        half = dot(w, col, ((1,), (1,)))
        parts = []
        for k in range(4):
            part = half[:, k * SIDE : (k + 1) * SIDE].astype(BF16)
            part = jnp.concatenate([part, part], 0)
            parts.append(dot(row[k * SIDE : (k + 1) * SIDE], part))
        for v in range(2):
            scratch[v, pl.ds(4 * step + s, SIDE, stride=16), :] = jnp.concatenate(
                parts[2 * v : 2 * v + 2], 1
            )

    @pl.when(step == 3)
    def _():
        for v in range(2):
            out_ref[:, :, v * 128 : (v + 1) * 128] = scratch[v].reshape(SIDE, 16, 128).astype(BF16)


def cloud_kernel(x_ref, factor_ref, w_in_ref, w_hidden_ref, w_out_ref, out_ref):
    def silu_of_twice(u):
        return (u + u * jnp.tanh(u)).astype(BF16)

    x = jnp.concatenate([x_ref[b, 0] for b in range(4)], 0)
    hidden = silu_of_twice(dot(w_in_ref[...], x))
    for layer in range(2):
        hidden = silu_of_twice(dot(w_hidden_ref[layer], hidden))
    logits = dot(w_out_ref[...], hidden)[:1]
    out_ref[0] = (factor_ref[0] / (1.0 + jnp.exp(logits))).astype(BF16)


def merge_kernel(y_ref, w_ref, id_ref, out_ref, pick, pick_t, weight):
    entries = y_ref.shape[0]
    chunk = 512
    chunks = entries // chunk
    lane = lax.broadcasted_iota(jnp.int32, (chunk // 4, 128), 1)
    for i in range(chunks):
        span = slice(i * chunk, (i + 1) * chunk)
        tile = lax.broadcasted_iota(jnp.int32, (128, chunk), 0) & 63
        hit = jnp.where(id_ref[:, span] == tile, 1.0, 0.0)
        pick[:, span] = hit[:SIDE].astype(BF16)
        pick_t[span, :] = hit.T.astype(BF16)
        rows = slice(i * chunk // 4, (i + 1) * chunk // 4)
        for v in range(2):
            w = w_ref[rows, v * 128 : (v + 1) * 128].astype(F32)
            turned = pltpu.roll(w, 64, 1)
            weight[pl.ds(i * chunk + 2 * v, chunk // 4, stride=4), :] = jnp.where(lane < 64, w, turned)
            weight[pl.ds(i * chunk + 2 * v + 1, chunk // 4, stride=4), :] = jnp.where(
                lane < 64, turned, w
            )

    def totals(estimate, exact):
        top = bottom = 0.0
        if estimate is not None:
            high = estimate.astype(BF16)
            low = (estimate - high.astype(F32)).astype(BF16)
            stacked = jnp.concatenate([high, low], 0)
        for i in range(chunks):
            span = slice(i * chunk, (i + 1) * chunk)
            y = y_ref[span, :].astype(F32)
            w = weight[span, :]
            h = jnp.concatenate([w, w], 1)
            if estimate is not None:
                residual = y - dot(pick_t[span, :], stacked)
                h = h * huber_delta / jnp.maximum(jnp.abs(residual), huber_delta)
            hy = h * y
            picked = pick[:, span]
            h_high, hy_high = h.astype(BF16), hy.astype(BF16)
            top = top + dot(picked, hy_high)
            bottom = bottom + dot(picked, h_high)
            if exact:
                top = top + dot(picked, (hy - hy_high.astype(F32)).astype(BF16))
                bottom = bottom + dot(picked, (h - h_high.astype(F32)).astype(BF16))
        return top / (bottom + prior_weight)

    estimate = totals(None, False)
    estimate = lax.fori_loop(0, HUBER_ITERS - 1, lambda _, e: totals(e, False), estimate)
    estimate = totals(estimate, True)

    lane = lax.broadcasted_iota(jnp.int32, (SIDE, 128), 1)
    for v in range(2):
        own = estimate[:, v * 128 : (v + 1) * 128]
        turned = pltpu.roll(own, 64, 1)
        for odd in range(2):
            first, second = (turned, own) if odd else (own, turned)
            after = pltpu.roll(second, SIDE - 1, 0)
            before = pltpu.roll(second, 1, 0)
            out_ref[:, 2 * v + odd, :] = jnp.where(
                lane < 64, first, jnp.where(lane < 96, after, before)
            )


def smooth_kernel(tile_ref, g_ref, out_ref):
    first = tile_ref[0] == 0
    last = tile_ref[0] == tile_ref[1] - 1
    lane = lax.broadcasted_iota(jnp.int32, (SIDE, 128), 1)
    row = lax.broadcasted_iota(jnp.int32, (SIDE, 128), 0)
    closed = ((lane == 127) & first) | ((lane == SIDE - 1) & last)
    bottom = row == SIDE - 1

    def flux(d):
        return d / (1.0 + d * d)

    for c in range(4):
        g = g_ref[:, c, :]
        for repeat in range(SMOOTH):
            across = jnp.where(closed, 0.0, flux(pltpu.roll(g, 127, 1) - g))
            down = jnp.where(bottom, 0.0, flux(pltpu.roll(g, SIDE - 1, 0) - g))
            g = g + smooth_rate * (
                across - pltpu.roll(across, 1, 1) + (down - pltpu.roll(down, 1, 0))
            )
        out_ref[c] = g[:, :SIDE]


def two_rows_per_line(x):
    scenes, planes, _ = x.shape
    x = x.reshape(scenes, planes, SIDE // 2, 128)
    return x.transpose(0, 2, 1, 3).reshape(scenes, planes * SIDE // 2, 128)


def whole(shape):
    return pl.BlockSpec(shape, lambda *_: (0,) * len(shape))


def per_device(
    granules,
    valid_rows,
    scene_order,
    intersections,
    row_resample,
    col_resample,
    w_in,
    w_hidden,
    w_out,
):
    scenes, bands, pixels = granules.shape
    tiles = lax.axis_size("tile")
    groups = lax.axis_size("band")
    share = scenes // groups
    spread = jnp.asarray(spread_matrix(4), BF16)
    spread1 = jnp.asarray(spread_matrix(1), BF16)

    by_scene = lax.all_to_all(
        granules.reshape(groups, share, bands, pixels), "band", split_axis=0, concat_axis=0
    )

    cols = two_rows_per_line(col_resample)
    rows = two_rows_per_line(row_resample)
    scene_block = pl.BlockSpec((4, 128, 128), lambda i: (i, 0, 0))
    moved = pl.pallas_call(
        reproject_kernel,
        grid=(4,),
        in_specs=[scene_block, scene_block, scene_block, whole((256, 128))],
        out_specs=pl.BlockSpec((SIDE, 16, 256), lambda i: (0, i, 0)),
        out_shape=jax.ShapeDtypeStruct((SIDE, 64, 256), BF16),
        scratch_shapes=[pltpu.VMEM((2, SIDE * 16, 128), F32)],
        name="reproject",
    )(two_rows_per_line(granules), cols, rows, spread)
    values = lax.all_to_all(moved, "tile", split_axis=0, concat_axis=0)

    ids = jnp.broadcast_to(intersections.reshape(1, 1, scenes * 4), (tiles, 1, scenes * 4))
    ids = lax.all_to_all(ids, "tile", split_axis=0, concat_axis=0).reshape(1, tiles * scenes * 4)

    first_scene = lax.axis_index("band") * share
    recency = jnp.exp(1.4 * scene_order.astype(F32) / (scenes * tiles) - 0.7)
    factor = valid_rows.astype(F32) * recency[:, None]
    factor = lax.dynamic_slice_in_dim(factor, first_scene, share, 0)
    factor = jnp.broadcast_to(factor[:, :, None], (share, SIDE, SIDE)).reshape(share, 1, pixels)
    half = jnp.asarray(0.5, BF16)
    width = 2048
    weights = pl.pallas_call(
        cloud_kernel,
        grid=(share, pixels // width),
        in_specs=[
            pl.BlockSpec((groups, 1, bands, width), lambda s, i: (0, s, 0, i)),
            pl.BlockSpec((1, 1, width), lambda s, i: (s, 0, i)),
            whole((256, 16)),
            whole((2, 256, 256)),
            whole((8, 256)),
        ],
        out_specs=pl.BlockSpec((1, 1, width), lambda s, i: (s, 0, i)),
        out_shape=jax.ShapeDtypeStruct((share, 1, pixels), BF16),
        name="cloud",
    )(
        by_scene,
        factor,
        w_in.T * half,
        w_hidden.transpose(0, 2, 1) * half,
        jnp.broadcast_to(w_out[None, :], (8, 256)),
    )
    weights = weights.reshape(1, share * SIDE // 2, 128)
    weights = lax.all_to_all(
        jnp.broadcast_to(weights, (groups,) + weights.shape[1:]), "band", split_axis=0, concat_axis=0
    ).reshape(scenes, SIDE // 2, 128)
    moved_weights = pl.pallas_call(
        weight_kernel,
        grid=(4,),
        in_specs=[
            pl.BlockSpec((4, SIDE // 2, 128), lambda i: (i, 0, 0)),
            scene_block,
            scene_block,
            whole((256, 128)),
            whole((SIDE, SIDE // 2)),
        ],
        out_specs=whole((SIDE, scenes, 256)),
        out_shape=jax.ShapeDtypeStruct((SIDE, scenes, 256), BF16),
        scratch_shapes=[pltpu.VMEM((2, SIDE * 16, 128), F32)],
        name="reproject_weights",
    )(weights, cols, rows, spread, spread1)
    moved_weights = lax.all_to_all(moved_weights, "tile", split_axis=0, concat_axis=0)

    entries = tiles * scenes * 4
    estimate = pl.pallas_call(
        merge_kernel,
        out_shape=jax.ShapeDtypeStruct((tiles, 4, 128), F32),
        scratch_shapes=[
            pltpu.VMEM((SIDE, entries), BF16),
            pltpu.VMEM((entries, 128), BF16),
            pltpu.VMEM((entries, 128), F32),
        ],
        name="merge",
    )(values.reshape(entries, 256), moved_weights.reshape(tiles * scenes, 256), ids)
    field = lax.all_to_all(estimate, "tile", split_axis=0, concat_axis=0)

    place = jnp.stack([lax.axis_index("tile"), tiles]).astype(jnp.int32)
    out = pl.pallas_call(
        smooth_kernel,
        in_specs=[pl.BlockSpec(memory_space=pltpu.SMEM), whole((SIDE, 4, 128))],
        out_specs=whole((4, SIDE, SIDE)),
        out_shape=jax.ShapeDtypeStruct((4, SIDE, SIDE), F32),
        name="smooth",
    )(place, field)
    return out.reshape(4, pixels)


def solution(mesh):
    return jax.shard_map(
        per_device,
        mesh=mesh,
        in_specs=(
            P("tile", "band", None),
            P("tile", None),
            P("tile"),
            P("tile", None),
            P("tile", None, None),
            P("tile", None, None),
            P(),
            P(),
            P(),
        ),
        out_specs=P("band", "tile"),
        check_vma=False,
    )
```

```python
import jax
import jax.numpy as jnp
import numpy as np
from jax import lax
from jax.experimental import pallas as pl
from jax.experimental.pallas import tpu as pltpu
from jax.sharding import PartitionSpec as P

HUBER_ITERS = 4
SMOOTH = 2

prior_weight = 0.25
huber_delta = 0.5
smooth_rate = 0.2

F32 = jnp.float32
BF16 = jnp.bfloat16
SIDE = 64


def dot(a, b, contract=((1,), (0,))):
    return lax.dot_general(a, b, (contract, ((), ())), preferred_element_type=F32)


def spread_matrix(count):
    out = np.zeros((count * SIDE, count * SIDE // 2), np.float32)
    for a in range(count):
        for i in range(SIDE):
            out[a * SIDE + i, count * (i // 2) + a] = 1.0
    return out


def parity_mask(rows):
    row = lax.broadcasted_iota(jnp.int32, (rows, 128), 0)
    lane = lax.broadcasted_iota(jnp.int32, (rows, 128), 1)
    return (row & 1) == (lane >> 6)


def spread_pair(both, mask):
    col = jnp.where(mask, both[:, :128], 0.0)
    col = (col + pltpu.roll(col, 64, 1)).astype(BF16)
    row = jnp.where(mask, both[:, 128:], 0.0).astype(BF16)
    return col, row


def reproject_kernel(x_ref, col_ref, row_ref, spread_ref, out_ref, scratch):
    mask = parity_mask(256)
    spread = spread_ref[...]
    group = range(4)
    wide = [jnp.concatenate([x_ref[s], col_ref[s], row_ref[s]], 1) for s in group]
    wide = [dot(spread, w) for w in wide]
    planes = [jnp.where(mask, w[:, :128], 0.0).astype(BF16) for w in wide]
    pairs = [spread_pair(w[:, 128:], mask) for w in wide]
    halves = [dot(planes[s], pairs[s][0], ((1,), (1,))) for s in group]
    for s in group:
        for k in range(4):
            lanes = slice(k * SIDE, (k + 1) * SIDE)
            part = [halves[s][c * SIDE : (c + 1) * SIDE, lanes] for c in range(4)]
            part = jnp.concatenate(part, 1).astype(BF16)
            part = jnp.concatenate([part, part], 0)
            moved = dot(pairs[s][1][k * SIDE : (k + 1) * SIDE], part)
            for v in range(2):
                scratch[v, pl.ds(4 * k + s, SIDE, stride=16), :] = moved[:, v * 128 : (v + 1) * 128]
    for v in range(2):
        out_ref[:, :, v * 128 : (v + 1) * 128] = scratch[v].reshape(SIDE, 16, 128).astype(BF16)


def weight_kernel(
    band_ref, w_ref, id_ref, col_ref, row_ref, spread_ref, spread1_ref, out_ref, scratch
):
    mask = parity_mask(256)
    mask1 = parity_mask(SIDE)
    spread = spread_ref[...]
    spread1 = spread1_ref[...]
    group = range(4)
    planes = [jnp.where(mask1, dot(spread1, w_ref[s]), 0.0).astype(BF16) for s in group]
    wide = [dot(spread, jnp.concatenate([col_ref[s], row_ref[s]], 1)) for s in group]
    pairs = [spread_pair(w, mask) for w in wide]
    halves = [dot(planes[s], pairs[s][0], ((1,), (1,))) for s in group]
    for s in group:
        parts = []
        for k in range(4):
            part = halves[s][:, k * SIDE : (k + 1) * SIDE].astype(BF16)
            part = jnp.concatenate([part, part], 0)
            parts.append(dot(pairs[s][1][k * SIDE : (k + 1) * SIDE], part))
        for v in range(2):
            pair = jnp.concatenate(parts[2 * v : 2 * v + 2], 1)
            scratch[v, pl.ds(s, SIDE, stride=4), :] = pair
    for v in range(2):
        out_ref[:, v] = scratch[v].reshape(SIDE, 4, 128).astype(BF16)
    out_ref[:, 2] = jnp.broadcast_to(id_ref[...].astype(BF16)[None], (SIDE, 4, 128))


def cloud_kernel(x0, x1, x2, x3, factor_ref, w_in_ref, w_hidden_ref, w_out_ref, out_ref):
    def silu_of_twice(u):
        return (u + u * jnp.tanh(u)).astype(BF16)

    scene, width = pl.program_id(0), factor_ref.shape[2]
    lanes = pl.ds(pl.multiple_of(pl.program_id(1) * width, width), width)
    x = jnp.concatenate([x_ref[scene, :, lanes] for x_ref in (x0, x1, x2, x3)], 0)
    hidden = silu_of_twice(dot(w_in_ref[...], x))
    for layer in range(2):
        hidden = silu_of_twice(dot(w_hidden_ref[layer], hidden))
    logits = dot(w_out_ref[...], hidden)[:1]
    weight = factor_ref[0] / (1.0 + jnp.exp(logits))
    lines = [weight[:, i * 128 : (i + 1) * 128] for i in range(weight.shape[1] // 128)]
    out_ref[0] = jnp.concatenate(lines, 0).astype(BF16)


def merge_kernel(y_ref, w_ref, out_ref, pick, pick_t, weight):
    entries = y_ref.shape[0]
    chunk = 512
    chunks = entries // chunk
    lane = lax.broadcasted_iota(jnp.int32, (entries // SIDE, 128), 1)
    tile = (lax.broadcasted_iota(jnp.int32, (128, 128), 0) & 63).astype(F32)
    ids = w_ref[0, :, 2].astype(F32)[:, 0, :]
    turned = pltpu.roll(ids, 64, 1)
    for i in range(entries // 128):
        span = slice(i * 128, (i + 1) * 128)
        pair = jnp.where(lane[:1] < 64, ids[2 * i : 2 * i + 1], turned[2 * i + 1 : 2 * i + 2])
        hit = jnp.where(pair == tile, 1.0, 0.0)
        pick[:, span] = hit[:SIDE].astype(BF16)
        pick_t[span, :] = hit.T.astype(BF16)
    lane = lax.broadcasted_iota(jnp.int32, (entries // SIDE, 4, 128), 2)
    for b in range(4):
        for v in range(2):
            w = w_ref[b, :, v].astype(F32) * huber_delta
            turned = pltpu.roll(w, 64, 2)
            first = 16 * b + 8 * v
            weight[:, first : first + 4, :] = jnp.where(lane < 64, w, turned)
            weight[:, first + 4 : first + 8, :] = jnp.where(lane < 64, turned, w)

    def totals(estimate, exact):
        top = bottom = 0.0
        if estimate is not None:
            high = estimate.astype(BF16)
            low = (estimate - high.astype(F32)).astype(BF16)
            stacked = jnp.concatenate([high, low], 0)
        for i in range(chunks):
            span = slice(i * chunk, (i + 1) * chunk)
            y = y_ref[span, :].astype(F32)
            w = weight[i * chunk // SIDE : (i + 1) * chunk // SIDE].reshape(chunk, 128)
            if estimate is None:
                h = jnp.concatenate([w, w], 1) * (1.0 / huber_delta)
            else:
                residual = y - dot(pick_t[span, :], stacked)
                h = jnp.concatenate([w, w], 1) / jnp.maximum(jnp.abs(residual), huber_delta)
            hy = h * y
            picked = pick[:, span]
            h_high, hy_high = h.astype(BF16), hy.astype(BF16)
            top = top + dot(picked, hy_high)
            bottom = bottom + dot(picked, h_high)
            if exact:
                top = top + dot(picked, (hy - hy_high.astype(F32)).astype(BF16))
                bottom = bottom + dot(picked, (h - h_high.astype(F32)).astype(BF16))
        return top / (bottom + prior_weight)

    estimate = totals(None, False)
    estimate = lax.fori_loop(0, HUBER_ITERS - 1, lambda _, e: totals(e, False), estimate)
    estimate = totals(estimate, True)

    lane = lax.broadcasted_iota(jnp.int32, (SIDE, 128), 1)
    for v in range(2):
        own = estimate[:, v * 128 : (v + 1) * 128]
        turned = pltpu.roll(own, 64, 1)
        for odd in range(2):
            first, second = (turned, own) if odd else (own, turned)
            after = pltpu.roll(second, SIDE - 1, 0)
            before = pltpu.roll(second, 1, 0)
            out_ref[:, 2 * v + odd, :] = jnp.where(
                lane < 64, first, jnp.where(lane < 96, after, before)
            )


def smooth_kernel(tile_ref, g_ref, out_ref, scratch):
    first = tile_ref[0] == 0
    last = tile_ref[0] == tile_ref[1] - 1
    lane = lax.broadcasted_iota(jnp.int32, (SIDE, 128), 1)
    row = lax.broadcasted_iota(jnp.int32, (SIDE, 128), 0)
    closed = ((lane == 127) & first) | ((lane == SIDE - 1) & last)
    bottom = row == SIDE - 1

    def flux(d):
        return d / (1.0 + d * d)

    for c in range(4):
        g = g_ref[:, c, :]
        for repeat in range(SMOOTH):
            across = jnp.where(closed, 0.0, flux(pltpu.roll(g, 127, 1) - g))
            down = jnp.where(bottom, 0.0, flux(pltpu.roll(g, SIDE - 1, 0) - g))
            g = g + smooth_rate * (
                across - pltpu.roll(across, 1, 1) + (down - pltpu.roll(down, 1, 0))
            )
        scratch[c] = g
        even = scratch[c, pl.ds(0, SIDE // 2, stride=2), :]
        odd = scratch[c, pl.ds(1, SIDE // 2, stride=2), :]
        out_ref[:, c, :] = jnp.where(lane[: SIDE // 2] < SIDE, even, pltpu.roll(odd, SIDE, 1))


def two_rows_per_line(x):
    scenes, planes, _ = x.shape
    x = x.reshape(scenes, planes, SIDE // 2, 128)
    return x.transpose(0, 2, 1, 3).reshape(scenes, planes * SIDE // 2, 128)


def keep(x):
    return pltpu.with_memory_space_constraint(x, pltpu.VMEM)


def whole(shape):
    return pl.BlockSpec(shape, lambda *_: (0,) * len(shape))


def per_device(
    granules,
    valid_rows,
    scene_order,
    intersections,
    row_resample,
    col_resample,
    w_in,
    w_hidden,
    w_out,
):
    scenes, bands, pixels = granules.shape
    tiles = lax.axis_size("tile")
    groups = lax.axis_size("band")
    share = scenes // groups
    spread = jnp.asarray(spread_matrix(4), BF16)
    spread1 = jnp.asarray(spread_matrix(1), BF16)

    in_vmem = pl.BlockSpec(memory_space=pltpu.VMEM)
    cols = two_rows_per_line(col_resample)
    rows = two_rows_per_line(row_resample)
    scene_block = pl.BlockSpec((4, 128, 128), lambda i: (i, 0, 0))
    moved = pl.pallas_call(
        reproject_kernel,
        grid=(4,),
        in_specs=[scene_block, scene_block, scene_block, whole((256, 128))],
        out_specs=pl.BlockSpec((SIDE, 16, 256), lambda i: (0, i, 0)),
        out_shape=jax.ShapeDtypeStruct((SIDE, 64, 256), BF16),
        scratch_shapes=[pltpu.VMEM((2, SIDE * 16, 128), F32)],
        name="reproject",
    )(two_rows_per_line(granules), cols, rows, spread)
    moved, granules = lax.optimization_barrier((moved, granules))
    values = lax.all_to_all(moved, "tile", split_axis=0, concat_axis=0)

    band = lax.axis_index("band")
    by_group = granules.reshape(groups, share, bands, pixels)
    w_in = w_in.reshape(groups, bands, -1)
    layers, w_rows = [], []
    for turn in range(groups):
        part = lax.dynamic_index_in_dim(by_group, (band + turn) % groups, 0, keepdims=False)
        if turn:
            part = lax.ppermute(part, "band", [(i, (i + turn) % groups) for i in range(groups)])
        layers.append(part)
        w_rows.append(lax.dynamic_index_in_dim(w_in, (band - turn) % groups, 0, keepdims=False))
    w_in = jnp.concatenate(w_rows, 0)

    first_scene = band * share
    recency = jnp.exp(1.4 * scene_order.astype(F32) / (scenes * tiles) - 0.7)
    factor = valid_rows.astype(F32) * recency[:, None]
    factor = lax.dynamic_slice_in_dim(factor, first_scene, share, 0)
    factor = jnp.broadcast_to(factor[:, :, None], (share, SIDE, SIDE)).reshape(share, 1, pixels)
    half = jnp.asarray(0.5, BF16)
    width = 2048
    weights = pl.pallas_call(
        cloud_kernel,
        grid=(share, pixels // width),
        in_specs=[in_vmem] * groups
        + [
            pl.BlockSpec((1, 1, width), lambda s, i: (s, 0, i)),
            whole((256, 16)),
            whole((2, 256, 256)),
            whole((8, 256)),
        ],
        out_specs=pl.BlockSpec((1, width // 128, 128), lambda s, i: (s, i, 0)),
        out_shape=jax.ShapeDtypeStruct((share, SIDE // 2, 128), BF16),
        cost_estimate=pl.CostEstimate(flops=12 * 10**9, transcendentals=0, bytes_accessed=10**6),
        name="cloud",
    )(
        *map(keep, layers),
        factor,
        w_in.T * half,
        w_hidden.transpose(0, 2, 1) * half,
        jnp.broadcast_to(w_out[None, :], (8, 256)),
    )
    ids = intersections.reshape(groups, share, 4).transpose(0, 2, 1).reshape(1, scenes * 4)
    ids = jnp.broadcast_to(jnp.pad(ids, ((0, 0), (0, 128 - scenes * 4))).astype(F32), (4, 128))
    mine = pl.BlockSpec((4, 128, 128), lambda i, b: (b[0], 0, 0))
    moved_weights = pl.pallas_call(
        weight_kernel,
        grid_spec=pltpu.PrefetchScalarGridSpec(
            num_scalar_prefetch=1,
            grid=(1,),
            in_specs=[
                whole((share, SIDE // 2, 128)),
                whole((4, 128)),
                mine,
                mine,
                whole((256, 128)),
                whole((SIDE, SIDE // 2)),
            ],
            out_specs=whole((SIDE, 3, share, 128)),
            scratch_shapes=[pltpu.VMEM((2, SIDE * share, 128), F32)],
        ),
        out_shape=jax.ShapeDtypeStruct((SIDE, 3, share, 128), BF16),
        name="reproject_weights",
    )(band.astype(jnp.int32).reshape(1), weights, ids, cols, rows, spread, spread1)
    moved_weights, values = lax.optimization_barrier((moved_weights, values))
    moved_weights = lax.all_to_all(moved_weights, "tile", split_axis=0, concat_axis=0)
    moved_weights = jnp.broadcast_to(moved_weights[None], (groups,) + moved_weights.shape)
    moved_weights = lax.all_to_all(moved_weights, "band", split_axis=0, concat_axis=0)

    entries = tiles * scenes * 4
    estimate = pl.pallas_call(
        merge_kernel,
        in_specs=[in_vmem, in_vmem],
        out_shape=jax.ShapeDtypeStruct((tiles, 4, 128), F32),
        scratch_shapes=[
            pltpu.VMEM((SIDE, entries), BF16),
            pltpu.VMEM((entries, 128), BF16),
            pltpu.VMEM((tiles, SIDE, 128), F32),
        ],
        name="merge",
    )(keep(values.reshape(entries, 256)), keep(moved_weights))
    field = lax.all_to_all(estimate, "tile", split_axis=0, concat_axis=0)

    place = jnp.stack([lax.axis_index("tile"), tiles]).astype(jnp.int32)
    out = pl.pallas_call(
        smooth_kernel,
        in_specs=[pl.BlockSpec(memory_space=pltpu.SMEM), in_vmem],
        out_shape=jax.ShapeDtypeStruct((SIDE // 2, 4, 128), F32),
        scratch_shapes=[pltpu.VMEM((4, SIDE, 128), F32)],
        name="smooth",
    )(place, keep(field))
    return out.transpose(1, 0, 2).reshape(4, pixels)


def solution(mesh):
    return jax.shard_map(
        per_device,
        mesh=mesh,
        in_specs=(
            P("tile", "band", None),
            P("tile", None),
            P("tile"),
            P("tile", None),
            P("tile", None, None),
            P("tile", None, None),
            P(),
            P(),
            P(),
        ),
        out_specs=P("band", "tile"),
        check_vma=False,
    )
```

```python
import jax
import jax.numpy as jnp
import numpy as np
from jax import lax
from jax.experimental import pallas as pl
from jax.experimental.pallas import tpu as pltpu
from jax.sharding import PartitionSpec as P

HUBER_ITERS = 4
SMOOTH = 2

prior_weight = 0.25
huber_delta = 0.5
smooth_rate = 0.2

F32 = jnp.float32
BF16 = jnp.bfloat16
SIDE = 64


def dot(a, b, contract=((1,), (0,))):
    return lax.dot_general(a, b, (contract, ((), ())), preferred_element_type=F32)


def spread_matrix(count):
    out = np.zeros((count * SIDE, count * SIDE // 2), np.float32)
    for a in range(count):
        for i in range(SIDE):
            out[a * SIDE + i, count * (i // 2) + a] = 1.0
    return out


def parity_mask(rows):
    row = lax.broadcasted_iota(jnp.int32, (rows, 128), 0)
    lane = lax.broadcasted_iota(jnp.int32, (rows, 128), 1)
    return (row & 1) == (lane >> 6)


def spread_pair(both, mask):
    col = jnp.where(mask, both[:, :128], 0.0)
    col = (col + pltpu.roll(col, 64, 1)).astype(BF16)
    row = jnp.where(mask, both[:, 128:], 0.0).astype(BF16)
    return col, row


def reproject_kernel(x_ref, col_ref, row_ref, spread_ref, out_ref, scratch):
    mask = parity_mask(256)
    spread = spread_ref[...]
    group = range(4)
    wide = [jnp.concatenate([x_ref[s], col_ref[s], row_ref[s]], 1) for s in group]
    wide = [dot(spread, w) for w in wide]
    planes = [jnp.where(mask, w[:, :128], 0.0).astype(BF16) for w in wide]
    pairs = [spread_pair(w[:, 128:], mask) for w in wide]
    halves = [dot(planes[s], pairs[s][0], ((1,), (1,))) for s in group]
    for s in group:
        for k in range(4):
            lanes = slice(k * SIDE, (k + 1) * SIDE)
            part = [halves[s][c * SIDE : (c + 1) * SIDE, lanes] for c in range(4)]
            part = jnp.concatenate(part, 1).astype(BF16)
            part = jnp.concatenate([part, part], 0)
            moved = dot(pairs[s][1][k * SIDE : (k + 1) * SIDE], part)
            for v in range(2):
                scratch[v, pl.ds(4 * k + s, SIDE, stride=16), :] = moved[:, v * 128 : (v + 1) * 128]
    for v in range(2):
        out_ref[:, :, v * 128 : (v + 1) * 128] = scratch[v].reshape(SIDE, 16, 128).astype(BF16)


def weight_kernel(
    band_ref, w0, w1, w2, w3, id_ref, col_ref, row_ref, spread_ref, spread1_ref, out_ref, scratch
):
    turn = pl.program_id(0)
    place = 2 * ((band_ref[0] + 4 - turn) % 4)
    mask = parity_mask(256)
    mask1 = parity_mask(SIDE)
    spread = spread_ref[...]
    spread1 = spread1_ref[...]
    group = range(4)
    w = jnp.where(turn < 2, jnp.where(turn < 1, w0[...], w1[...]), jnp.where(turn < 3, w2[...], w3[...]))
    planes = [jnp.where(mask1, dot(spread1, w[s]), 0.0).astype(BF16) for s in group]
    wide = [dot(spread, jnp.concatenate([col_ref[s], row_ref[s]], 1)) for s in group]
    pairs = [spread_pair(x, mask) for x in wide]
    halves = [dot(planes[s], pairs[s][0], ((1,), (1,))) for s in group]
    for s in group:
        parts = []
        for k in range(4):
            part = halves[s][:, k * SIDE : (k + 1) * SIDE].astype(BF16)
            part = jnp.concatenate([part, part], 0)
            parts.append(dot(pairs[s][1][k * SIDE : (k + 1) * SIDE], part))
        for v in range(2):
            pair = jnp.concatenate(parts[2 * v : 2 * v + 2], 1)
            scratch[v, pl.ds(s, SIDE, stride=4), :] = pair
    for v in range(2):
        out_ref[:, place + v] = scratch[v].reshape(SIDE, 4, 128).astype(BF16)

    @pl.when(turn == 0)
    def _():
        out_ref[:, 8] = jnp.broadcast_to(id_ref[...].astype(BF16)[None], (SIDE, 4, 128))


def after_kernel(x_ref, first_ref, out_ref):
    pass


def cloud_kernel(x0, x1, x2, x3, factor_ref, w_in_ref, w_hidden_ref, w_out_ref, out_ref):
    def silu_of_twice(u):
        return (u + u * jnp.tanh(u)).astype(BF16)

    scene, width = pl.program_id(0), factor_ref.shape[2]
    lanes = pl.ds(pl.multiple_of(pl.program_id(1) * width, width), width)
    x = jnp.concatenate([x_ref[scene, :, lanes] for x_ref in (x0, x1, x2, x3)], 0)
    hidden = silu_of_twice(dot(w_in_ref[...], x))
    for layer in range(2):
        hidden = silu_of_twice(dot(w_hidden_ref[layer], hidden))
    logits = dot(w_out_ref[...], hidden)[:1]
    weight = factor_ref[0] / (1.0 + jnp.exp(logits))
    lines = [weight[:, i * 128 : (i + 1) * 128] for i in range(weight.shape[1] // 128)]
    out_ref[0] = jnp.concatenate(lines, 0).astype(BF16)


def merge_kernel(y_in, w_ref, out_ref, y_ref, pick, pick_t, weight, arrival):
    fetch = pltpu.make_async_copy(y_in, y_ref, arrival)
    fetch.start()
    entries = y_ref.shape[0]
    chunk = 512
    chunks = entries // chunk
    lane = lax.broadcasted_iota(jnp.int32, (entries // SIDE, 128), 1)
    tile = (lax.broadcasted_iota(jnp.int32, (128, 128), 0) & 63).astype(F32)
    ids = w_ref[:, 8].astype(F32)[:, 0, :]
    turned = pltpu.roll(ids, 64, 1)
    for i in range(entries // 128):
        span = slice(i * 128, (i + 1) * 128)
        pair = jnp.where(lane[:1] < 64, ids[2 * i : 2 * i + 1], turned[2 * i + 1 : 2 * i + 2])
        hit = jnp.where(pair == tile, 1.0, 0.0)
        pick[:, span] = hit[:SIDE].astype(BF16)
        pick_t[span, :] = hit.T.astype(BF16)
    lane = lax.broadcasted_iota(jnp.int32, (entries // SIDE, 4, 128), 2)
    for b in range(4):
        for v in range(2):
            w = w_ref[:, 2 * b + v].astype(F32) * huber_delta
            turned = pltpu.roll(w, 64, 2)
            first = 16 * b + 8 * v
            weight[:, first : first + 4, :] = jnp.where(lane < 64, w, turned)
            weight[:, first + 4 : first + 8, :] = jnp.where(lane < 64, turned, w)

    fetch.wait()

    def totals(estimate, exact):
        top = bottom = 0.0
        if estimate is not None:
            high = estimate.astype(BF16)
            low = (estimate - high.astype(F32)).astype(BF16)
            stacked = jnp.concatenate([high, low], 0)
        for i in range(chunks):
            span = slice(i * chunk, (i + 1) * chunk)
            y = y_ref[span, :].astype(F32)
            w = weight[i * chunk // SIDE : (i + 1) * chunk // SIDE].reshape(chunk, 128)
            if estimate is None:
                h = jnp.concatenate([w, w], 1) * (1.0 / huber_delta)
            else:
                residual = y - dot(pick_t[span, :], stacked)
                h = jnp.concatenate([w, w], 1) / jnp.maximum(jnp.abs(residual), huber_delta)
            picked = pick[:, span]
            h_high = h.astype(BF16)
            if exact:
                hy = h * y
                hy_high = hy.astype(BF16)
            else:
                hy_high = h_high * y_ref[span, :]
            top = top + dot(picked, hy_high)
            bottom = bottom + dot(picked, h_high)
            if exact:
                top = top + dot(picked, (hy - hy_high.astype(F32)).astype(BF16))
                bottom = bottom + dot(picked, (h - h_high.astype(F32)).astype(BF16))
        return top / (bottom + prior_weight)

    estimate = totals(None, False)
    estimate = lax.fori_loop(0, HUBER_ITERS - 1, lambda _, e: totals(e, False), estimate)
    estimate = totals(estimate, True)

    lane = lax.broadcasted_iota(jnp.int32, (SIDE, 128), 1)
    for v in range(2):
        own = estimate[:, v * 128 : (v + 1) * 128]
        turned = pltpu.roll(own, 64, 1)
        for odd in range(2):
            first, second = (turned, own) if odd else (own, turned)
            after = pltpu.roll(second, SIDE - 1, 0)
            before = pltpu.roll(second, 1, 0)
            out_ref[:, 2 * v + odd, :] = jnp.where(
                lane < 64, first, jnp.where(lane < 96, after, before)
            )


def smooth_kernel(tile_ref, g_ref, out_ref, scratch):
    first = tile_ref[0] == 0
    last = tile_ref[0] == tile_ref[1] - 1
    lane = lax.broadcasted_iota(jnp.int32, (SIDE, 128), 1)
    row = lax.broadcasted_iota(jnp.int32, (SIDE, 128), 0)
    closed = ((lane == 127) & first) | ((lane == SIDE - 1) & last)
    bottom = row == SIDE - 1

    def flux(d):
        return d / (1.0 + d * d)

    for c in range(4):
        g = g_ref[:, c, :]
        for repeat in range(SMOOTH):
            across = jnp.where(closed, 0.0, flux(pltpu.roll(g, 127, 1) - g))
            down = jnp.where(bottom, 0.0, flux(pltpu.roll(g, SIDE - 1, 0) - g))
            g = g + smooth_rate * (
                across - pltpu.roll(across, 1, 1) + (down - pltpu.roll(down, 1, 0))
            )
        scratch[c] = g
        even = scratch[c, pl.ds(0, SIDE // 2, stride=2), :]
        odd = scratch[c, pl.ds(1, SIDE // 2, stride=2), :]
        out_ref[:, c, :] = jnp.where(lane[: SIDE // 2] < SIDE, even, pltpu.roll(odd, SIDE, 1))


def two_rows_per_line(x):
    scenes, planes, _ = x.shape
    x = x.reshape(scenes, planes, SIDE // 2, 128)
    return x.transpose(0, 2, 1, 3).reshape(scenes, planes * SIDE // 2, 128)


def keep(x):
    return pltpu.with_memory_space_constraint(x, pltpu.VMEM)


def whole(shape):
    return pl.BlockSpec(shape, lambda *_: (0,) * len(shape))


def per_device(
    granules,
    valid_rows,
    scene_order,
    intersections,
    row_resample,
    col_resample,
    w_in,
    w_hidden,
    w_out,
):
    scenes, bands, pixels = granules.shape
    tiles = lax.axis_size("tile")
    groups = lax.axis_size("band")
    share = scenes // groups
    spread = jnp.asarray(spread_matrix(4), BF16)
    spread1 = jnp.asarray(spread_matrix(1), BF16)

    in_vmem = pl.BlockSpec(memory_space=pltpu.VMEM)
    cols = two_rows_per_line(col_resample)
    rows = two_rows_per_line(row_resample)
    scene_block = pl.BlockSpec((4, 128, 128), lambda i: (i, 0, 0))
    moved = pl.pallas_call(
        reproject_kernel,
        grid=(4,),
        in_specs=[scene_block, scene_block, scene_block, whole((256, 128))],
        out_specs=pl.BlockSpec((SIDE, 16, 256), lambda i: (0, i, 0)),
        out_shape=jax.ShapeDtypeStruct((SIDE, 64, 256), BF16),
        scratch_shapes=[pltpu.VMEM((2, SIDE * 16, 128), F32)],
        name="reproject",
    )(two_rows_per_line(granules), cols, rows, spread)
    moved, granules = lax.optimization_barrier((moved, granules))
    values = lax.all_to_all(moved, "tile", split_axis=0, concat_axis=0)

    band = lax.axis_index("band")
    by_group = granules.reshape(groups, share, bands, pixels)
    w_in = w_in.reshape(groups, bands, -1)
    layers, w_rows = [], []
    for turn in range(groups):
        part = lax.dynamic_index_in_dim(by_group, (band + turn) % groups, 0, keepdims=False)
        if turn:
            part = lax.ppermute(part, "band", [(i, (i + turn) % groups) for i in range(groups)])
        layers.append(part)
        w_rows.append(lax.dynamic_index_in_dim(w_in, (band - turn) % groups, 0, keepdims=False))
    w_in = jnp.concatenate(w_rows, 0)

    first_scene = band * share
    recency = jnp.exp(1.4 * scene_order.astype(F32) / (scenes * tiles) - 0.7)
    factor = valid_rows.astype(F32) * recency[:, None]
    factor = lax.dynamic_slice_in_dim(factor, first_scene, share, 0)
    factor = jnp.broadcast_to(factor[:, :, None], (share, SIDE, SIDE)).reshape(share, 1, pixels)
    half = jnp.asarray(0.5, BF16)
    width = 2048
    weights = pl.pallas_call(
        cloud_kernel,
        grid=(share, pixels // width),
        in_specs=[in_vmem] * groups
        + [
            pl.BlockSpec((1, 1, width), lambda s, i: (s, 0, i)),
            whole((256, 16)),
            whole((2, 256, 256)),
            whole((8, 256)),
        ],
        out_specs=pl.BlockSpec((1, width // 128, 128), lambda s, i: (s, i, 0)),
        out_shape=jax.ShapeDtypeStruct((share, SIDE // 2, 128), BF16),
        cost_estimate=pl.CostEstimate(flops=12 * 10**9, transcendentals=0, bytes_accessed=10**6),
        name="cloud",
    )(
        *map(keep, layers),
        factor,
        w_in.T * half,
        w_hidden.transpose(0, 2, 1) * half,
        jnp.broadcast_to(w_out[None, :], (8, 256)),
    )
    ids = intersections.reshape(groups, share, 4).transpose(0, 2, 1).reshape(1, scenes * 4)
    ids = jnp.broadcast_to(jnp.pad(ids, ((0, 0), (0, 128 - scenes * 4))).astype(F32), (4, 128))
    all_weights = [weights] + [
        lax.ppermute(weights, "band", [(i, (i + turn) % groups) for i in range(groups)])
        for turn in range(1, groups)
    ]
    theirs = pl.BlockSpec((4, 128, 128), lambda i, b: ((b[0] + 4 - i) % 4, 0, 0))
    moved_weights = pl.pallas_call(
        weight_kernel,
        grid_spec=pltpu.PrefetchScalarGridSpec(
            num_scalar_prefetch=1,
            grid=(groups,),
            in_specs=[whole((share, SIDE // 2, 128))] * groups
            + [whole((4, 128)), theirs, theirs, whole((256, 128)), whole((SIDE, SIDE // 2))],
            out_specs=whole((SIDE, 9, share, 128)),
            scratch_shapes=[pltpu.VMEM((2, SIDE * share, 128), F32)],
        ),
        out_shape=jax.ShapeDtypeStruct((SIDE, 9, share, 128), BF16),
        cost_estimate=pl.CostEstimate(flops=8 * 10**9, transcendentals=0, bytes_accessed=10**6),
        name="reproject_weights",
    )(band.astype(jnp.int32).reshape(1), *all_weights, ids, cols, rows, spread, spread1)
    anywhere = pl.BlockSpec(memory_space=pl.ANY)
    moved_weights = pl.pallas_call(
        after_kernel,
        in_specs=[anywhere, anywhere],
        out_specs=anywhere,
        out_shape=jax.ShapeDtypeStruct(moved_weights.shape, BF16),
        input_output_aliases={0: 0},
        name="after",
    )(moved_weights, keep(values))
    moved_weights = lax.all_to_all(moved_weights, "tile", split_axis=0, concat_axis=0)

    entries = tiles * scenes * 4
    estimate = pl.pallas_call(
        merge_kernel,
        in_specs=[anywhere, in_vmem],
        out_shape=jax.ShapeDtypeStruct((tiles, 4, 128), F32),
        scratch_shapes=[
            pltpu.VMEM((entries, 256), BF16),
            pltpu.VMEM((SIDE, entries), BF16),
            pltpu.VMEM((entries, 128), BF16),
            pltpu.VMEM((tiles, SIDE, 128), F32),
            pltpu.SemaphoreType.DMA,
        ],
        name="merge",
    )(values.reshape(entries, 256), keep(moved_weights))
    field = lax.all_to_all(estimate, "tile", split_axis=0, concat_axis=0)

    place = jnp.stack([lax.axis_index("tile"), tiles]).astype(jnp.int32)
    out = pl.pallas_call(
        smooth_kernel,
        in_specs=[pl.BlockSpec(memory_space=pltpu.SMEM), in_vmem],
        out_shape=jax.ShapeDtypeStruct((SIDE // 2, 4, 128), F32),
        scratch_shapes=[pltpu.VMEM((4, SIDE, 128), F32)],
        name="smooth",
    )(place, keep(field))
    return out.transpose(1, 0, 2).reshape(4, pixels)


def solution(mesh):
    return jax.shard_map(
        per_device,
        mesh=mesh,
        in_specs=(
            P("tile", "band", None),
            P("tile", None),
            P("tile"),
            P("tile", None),
            P("tile", None, None),
            P("tile", None, None),
            P(),
            P(),
            P(),
        ),
        out_specs=P("band", "tile"),
        check_vma=False,
    )
```

```python
import jax
import jax.numpy as jnp
import numpy as np
from jax import lax
from jax.experimental import pallas as pl
from jax.experimental.pallas import tpu as pltpu
from jax.sharding import PartitionSpec as P

HUBER_ITERS = 4
SMOOTH = 2

prior_weight = 0.25
huber_delta = 0.5
smooth_rate = 0.2

F32 = jnp.float32
BF16 = jnp.bfloat16
SIDE = 64


def dot(a, b, contract=((1,), (0,))):
    return lax.dot_general(a, b, (contract, ((), ())), preferred_element_type=F32)


def spread_matrix(count):
    out = np.zeros((count * SIDE, count * SIDE // 2), np.float32)
    for a in range(count):
        for i in range(SIDE):
            out[a * SIDE + i, count * (i // 2) + a] = 1.0
    return out


def double_matrix():
    eye = huber_delta * np.eye(SIDE, dtype=np.float32)
    return np.kron(np.eye(2, dtype=np.float32), np.concatenate([eye, eye], 1))


def parity_mask(rows):
    row = lax.broadcasted_iota(jnp.int32, (rows, 128), 0)
    lane = lax.broadcasted_iota(jnp.int32, (rows, 128), 1)
    return (row & 1) == (lane >> 6)


def spread_pair(both, mask):
    col = jnp.where(mask, both[:, :128], 0.0).astype(BF16)
    col = col + pltpu.roll(col, 64, 1)
    row = jnp.where(mask, both[:, 128:], 0.0).astype(BF16)
    return col, row


def reproject_kernel(x_ref, col_ref, row_ref, spread_ref, out_ref, scratch):
    mask = parity_mask(256)
    spread = spread_ref[...]
    group = range(4)
    wide = [jnp.concatenate([x_ref[s], col_ref[s], row_ref[s]], 1) for s in group]
    wide = [dot(spread, w) for w in wide]
    planes = [jnp.where(mask, w[:, :128], 0.0).astype(BF16) for w in wide]
    pairs = [spread_pair(w[:, 128:], mask) for w in wide]
    halves = [dot(planes[s], pairs[s][0], ((1,), (1,))).astype(BF16) for s in group]
    for s in group:
        for k in range(4):
            lanes = slice(k * SIDE, (k + 1) * SIDE)
            part = [halves[s][c * SIDE : (c + 1) * SIDE, lanes] for c in range(4)]
            part = jnp.concatenate(part, 1)
            part = jnp.concatenate([part, part], 0)
            moved = dot(pairs[s][1][k * SIDE : (k + 1) * SIDE], part)
            for v in range(2):
                scratch[v, pl.ds(4 * k + s, SIDE, stride=16), :] = moved[:, v * 128 : (v + 1) * 128]
    for v in range(2):
        out_ref[:, :, v * 128 : (v + 1) * 128] = scratch[v].reshape(SIDE, 16, 128).astype(BF16)


def weight_kernel(
    band_ref, w0, w1, w2, w3, id_ref, col_ref, row_ref, spread_ref, spread1_ref, out_ref, scratch
):
    turn = pl.program_id(0)
    place = 2 * ((band_ref[0] + 4 - turn) % 4)
    mask = parity_mask(256)
    mask1 = parity_mask(SIDE)
    spread = spread_ref[...]
    spread1 = spread1_ref[...]
    group = range(4)
    w = jnp.where(turn < 2, jnp.where(turn < 1, w0[...], w1[...]), jnp.where(turn < 3, w2[...], w3[...]))
    planes = [jnp.where(mask1, dot(spread1, w[s]), 0.0).astype(BF16) for s in group]
    wide = [dot(spread, jnp.concatenate([col_ref[s], row_ref[s]], 1)) for s in group]
    pairs = [spread_pair(x, mask) for x in wide]
    halves = [dot(planes[s], pairs[s][0], ((1,), (1,))) for s in group]
    for s in group:
        parts = []
        for k in range(4):
            part = halves[s][:, k * SIDE : (k + 1) * SIDE].astype(BF16)
            part = jnp.concatenate([part, part], 0)
            parts.append(dot(pairs[s][1][k * SIDE : (k + 1) * SIDE], part))
        for v in range(2):
            pair = jnp.concatenate(parts[2 * v : 2 * v + 2], 1)
            scratch[v, pl.ds(s, SIDE, stride=4), :] = pair
    for v in range(2):
        out_ref[:, place + v] = scratch[v].reshape(SIDE, 4, 128).astype(BF16)

    @pl.when(turn == 0)
    def _():
        out_ref[:, 8] = jnp.broadcast_to(id_ref[...].astype(BF16)[None], (SIDE, 4, 128))


def after_kernel(x_ref, first_ref, out_ref):
    pass


def cloud_kernel(x0, x1, x2, x3, factor_ref, w_in_ref, w_hidden_ref, w_out_ref, out_ref):
    def silu_of_twice(u):
        return (u + u * jnp.tanh(u)).astype(BF16)

    scene, width = pl.program_id(0), factor_ref.shape[2]
    lanes = pl.ds(pl.multiple_of(pl.program_id(1) * width, width), width)
    x = jnp.concatenate([x_ref[scene, :, lanes] for x_ref in (x0, x1, x2, x3)], 0)
    hidden = silu_of_twice(dot(w_in_ref[...], x))
    for layer in range(2):
        hidden = silu_of_twice(dot(w_hidden_ref[layer], hidden))
    logits = dot(w_out_ref[...], hidden)[:1]
    weight = factor_ref[0] / (1.0 + jnp.exp(logits))
    lines = [weight[:, i * 128 : (i + 1) * 128] for i in range(weight.shape[1] // 128)]
    out_ref[0] = jnp.concatenate(lines, 0).astype(BF16)


def merge_kernel(y_in, w_ref, double_ref, out_ref, y_ref, pick, pick_t, weight, arrival):
    fetch = pltpu.make_async_copy(y_in, y_ref, arrival)
    fetch.start()
    entries = y_ref.shape[0]
    chunk = 512
    lane = lax.broadcasted_iota(jnp.int32, (1, 128), 1)
    tile = (lax.broadcasted_iota(jnp.int32, (128, 128), 0) & 63).astype(F32)
    ids = w_ref[:, 8].astype(F32)[:, 0, :]
    turned = pltpu.roll(ids, 64, 1)
    for i in range(entries // 128):
        span = slice(i * 128, (i + 1) * 128)
        pair = jnp.where(lane < 64, ids[2 * i : 2 * i + 1], turned[2 * i + 1 : 2 * i + 2])
        hit = jnp.where(pair == tile, 1.0, 0.0)
        pick[:, span] = hit[:SIDE].astype(BF16)
        pick_t[span, :] = hit.T.astype(BF16)
    for i in range(8):
        w = dot(w_ref[:, i].reshape(entries // 16, 128), double_ref[...])
        for half in range(2):
            first = 8 * i + 4 * half
            weight[:, first : first + 4, :] = w[:, half * 128 : (half + 1) * 128].reshape(
                entries // SIDE, 4, 128
            )
    fetch.wait()

    def totals(estimate):
        top = bottom = 0.0
        if estimate is not None:
            high = estimate.astype(BF16)
            low = (estimate - high.astype(F32)).astype(BF16)
            stacked = jnp.concatenate([high, low], 0)
        spans = [slice(i * chunk, (i + 1) * chunk) for i in range(entries // chunk)]

        def expected(span):
            return None if estimate is None else dot(pick_t[span, :], stacked)

        ahead = expected(spans[0])
        for i, span in enumerate(spans):
            here, ahead = ahead, expected(spans[i + 1]) if i + 1 < len(spans) else None
            w = weight[i * chunk // SIDE : (i + 1) * chunk // SIDE].reshape(chunk, 128)
            y = y_ref[span, :]
            h = jnp.concatenate([w, w], 1)
            if estimate is not None:
                h = h / jnp.maximum(jnp.abs(y.astype(F32) - here), huber_delta)
            h = h.astype(BF16)
            picked = pick[:, span]
            top = top + dot(picked, h * y)
            bottom = bottom + dot(picked, h)
        prior = prior_weight if estimate is not None else prior_weight * huber_delta
        return top / (bottom + prior)

    estimate = lax.fori_loop(0, HUBER_ITERS, lambda _, e: totals(e), totals(None))

    lane = lax.broadcasted_iota(jnp.int32, (SIDE, 128), 1)
    for v in range(2):
        own = estimate[:, v * 128 : (v + 1) * 128]
        turned = pltpu.roll(own, 64, 1)
        for odd in range(2):
            first, second = (turned, own) if odd else (own, turned)
            after = pltpu.roll(second, SIDE - 1, 0)
            before = pltpu.roll(second, 1, 0)
            out_ref[:, 2 * v + odd, :] = jnp.where(
                lane < 64, first, jnp.where(lane < 96, after, before)
            )


def smooth_kernel(tile_ref, g_ref, out_ref, scratch):
    first = tile_ref[0] == 0
    last = tile_ref[0] == tile_ref[1] - 1
    lane = lax.broadcasted_iota(jnp.int32, (SIDE, 128), 1)
    row = lax.broadcasted_iota(jnp.int32, (SIDE, 128), 0)
    closed = ((lane == 127) & first) | ((lane == SIDE - 1) & last)
    bottom = row == SIDE - 1

    def flux(d):
        return d / (1.0 + d * d)

    for c in range(4):
        g = g_ref[:, c, :]
        for repeat in range(SMOOTH):
            across = jnp.where(closed, 0.0, flux(pltpu.roll(g, 127, 1) - g))
            down = jnp.where(bottom, 0.0, flux(pltpu.roll(g, SIDE - 1, 0) - g))
            g = g + smooth_rate * (
                across - pltpu.roll(across, 1, 1) + (down - pltpu.roll(down, 1, 0))
            )
        scratch[c] = g
        even = scratch[c, pl.ds(0, SIDE // 2, stride=2), :]
        odd = scratch[c, pl.ds(1, SIDE // 2, stride=2), :]
        out_ref[:, c, :] = jnp.where(lane[: SIDE // 2] < SIDE, even, pltpu.roll(odd, SIDE, 1))


def two_rows_per_line(x):
    scenes, planes, _ = x.shape
    x = x.reshape(scenes, planes, SIDE // 2, 128)
    return x.transpose(0, 2, 1, 3).reshape(scenes, planes * SIDE // 2, 128)


def keep(x):
    return pltpu.with_memory_space_constraint(x, pltpu.VMEM)


def whole(shape):
    return pl.BlockSpec(shape, lambda *_: (0,) * len(shape))


def per_device(
    granules,
    valid_rows,
    scene_order,
    intersections,
    row_resample,
    col_resample,
    w_in,
    w_hidden,
    w_out,
):
    scenes, bands, pixels = granules.shape
    tiles = lax.axis_size("tile")
    groups = lax.axis_size("band")
    share = scenes // groups
    spread = jnp.asarray(spread_matrix(4), BF16)
    spread1 = jnp.asarray(spread_matrix(1), BF16)

    in_vmem = pl.BlockSpec(memory_space=pltpu.VMEM)
    cols = two_rows_per_line(col_resample)
    rows = two_rows_per_line(row_resample)
    scene_block = pl.BlockSpec((4, 128, 128), lambda i: (i, 0, 0))
    moved = pl.pallas_call(
        reproject_kernel,
        grid=(4,),
        in_specs=[scene_block, scene_block, scene_block, whole((256, 128))],
        out_specs=pl.BlockSpec((SIDE, 16, 256), lambda i: (0, i, 0)),
        out_shape=jax.ShapeDtypeStruct((SIDE, 64, 256), BF16),
        scratch_shapes=[pltpu.VMEM((2, SIDE * 16, 128), F32)],
        name="reproject",
    )(two_rows_per_line(granules), cols, rows, spread)
    moved, granules = lax.optimization_barrier((moved, granules))
    values = lax.all_to_all(moved, "tile", split_axis=0, concat_axis=0)

    band = lax.axis_index("band")
    by_group = granules.reshape(groups, share, bands, pixels)
    w_in = w_in.reshape(groups, bands, -1)
    layers, w_rows = [], []
    for turn in range(groups):
        part = lax.dynamic_index_in_dim(by_group, (band + turn) % groups, 0, keepdims=False)
        if turn:
            part = lax.ppermute(part, "band", [(i, (i + turn) % groups) for i in range(groups)])
        layers.append(part)
        w_rows.append(lax.dynamic_index_in_dim(w_in, (band - turn) % groups, 0, keepdims=False))
    w_in = jnp.concatenate(w_rows, 0)

    first_scene = band * share
    recency = jnp.exp(1.4 * scene_order.astype(F32) / (scenes * tiles) - 0.7)
    factor = valid_rows.astype(F32) * recency[:, None]
    factor = lax.dynamic_slice_in_dim(factor, first_scene, share, 0)
    factor = jnp.broadcast_to(factor[:, :, None], (share, SIDE, SIDE)).reshape(share, 1, pixels)
    half = jnp.asarray(0.5, BF16)
    width = 2048
    weights = pl.pallas_call(
        cloud_kernel,
        grid=(share, pixels // width),
        in_specs=[in_vmem] * groups
        + [
            pl.BlockSpec((1, 1, width), lambda s, i: (s, 0, i)),
            whole((256, 16)),
            whole((2, 256, 256)),
            whole((8, 256)),
        ],
        out_specs=pl.BlockSpec((1, width // 128, 128), lambda s, i: (s, i, 0)),
        out_shape=jax.ShapeDtypeStruct((share, SIDE // 2, 128), BF16),
        cost_estimate=pl.CostEstimate(flops=12 * 10**9, transcendentals=0, bytes_accessed=10**6),
        name="cloud",
    )(
        *map(keep, layers),
        factor,
        w_in.T * half,
        w_hidden.transpose(0, 2, 1) * half,
        jnp.broadcast_to(w_out[None, :], (8, 256)),
    )
    ids = intersections.reshape(groups, share, 4).transpose(0, 2, 1).reshape(1, scenes * 4)
    ids = jnp.broadcast_to(jnp.pad(ids, ((0, 0), (0, 128 - scenes * 4))).astype(F32), (4, 128))
    all_weights = [weights] + [
        lax.ppermute(weights, "band", [(i, (i + turn) % groups) for i in range(groups)])
        for turn in range(1, groups)
    ]
    theirs = pl.BlockSpec((4, 128, 128), lambda i, b: ((b[0] + 4 - i) % 4, 0, 0))
    moved_weights = pl.pallas_call(
        weight_kernel,
        grid_spec=pltpu.PrefetchScalarGridSpec(
            num_scalar_prefetch=1,
            grid=(groups,),
            in_specs=[whole((share, SIDE // 2, 128))] * groups
            + [whole((4, 128)), theirs, theirs, whole((256, 128)), whole((SIDE, SIDE // 2))],
            out_specs=whole((SIDE, 9, share, 128)),
            scratch_shapes=[pltpu.VMEM((2, SIDE * share, 128), F32)],
        ),
        out_shape=jax.ShapeDtypeStruct((SIDE, 9, share, 128), BF16),
        cost_estimate=pl.CostEstimate(flops=8 * 10**9, transcendentals=0, bytes_accessed=10**6),
        name="reproject_weights",
    )(band.astype(jnp.int32).reshape(1), *all_weights, ids, cols, rows, spread, spread1)
    anywhere = pl.BlockSpec(memory_space=pl.ANY)
    moved_weights = pl.pallas_call(
        after_kernel,
        in_specs=[anywhere, anywhere],
        out_specs=anywhere,
        out_shape=jax.ShapeDtypeStruct(moved_weights.shape, BF16),
        input_output_aliases={0: 0},
        name="after",
    )(moved_weights, keep(values))
    moved_weights = lax.all_to_all(moved_weights, "tile", split_axis=0, concat_axis=0)

    entries = tiles * scenes * 4
    estimate = pl.pallas_call(
        merge_kernel,
        in_specs=[anywhere, in_vmem, in_vmem],
        out_shape=jax.ShapeDtypeStruct((tiles, 4, 128), F32),
        scratch_shapes=[
            pltpu.VMEM((entries, 256), BF16),
            pltpu.VMEM((SIDE, entries), BF16),
            pltpu.VMEM((entries, 128), BF16),
            pltpu.VMEM((tiles, SIDE, 128), F32),
            pltpu.SemaphoreType.DMA,
        ],
        name="merge",
    )(values.reshape(entries, 256), keep(moved_weights), jnp.asarray(double_matrix(), BF16))
    field = lax.all_to_all(estimate, "tile", split_axis=0, concat_axis=0)

    place = jnp.stack([lax.axis_index("tile"), tiles]).astype(jnp.int32)
    out = pl.pallas_call(
        smooth_kernel,
        in_specs=[pl.BlockSpec(memory_space=pltpu.SMEM), in_vmem],
        out_shape=jax.ShapeDtypeStruct((SIDE // 2, 4, 128), F32),
        scratch_shapes=[pltpu.VMEM((4, SIDE, 128), F32)],
        name="smooth",
    )(place, keep(field))
    return out.transpose(1, 0, 2).reshape(4, pixels)


def solution(mesh):
    return jax.shard_map(
        per_device,
        mesh=mesh,
        in_specs=(
            P("tile", "band", None),
            P("tile", None),
            P("tile"),
            P("tile", None),
            P("tile", None, None),
            P("tile", None, None),
            P(),
            P(),
            P(),
        ),
        out_specs=P("band", "tile"),
        check_vma=False,
    )
```

```python
import jax
import jax.numpy as jnp
import numpy as np
from jax import lax
from jax.experimental import pallas as pl
from jax.experimental.pallas import tpu as pltpu
from jax.sharding import PartitionSpec as P

HUBER_ITERS = 4
SMOOTH = 2

prior_weight = 0.25
huber_delta = 0.5
smooth_rate = 0.2

F32 = jnp.float32
BF16 = jnp.bfloat16
SIDE = 64


def dot(a, b, contract=((1,), (0,))):
    return lax.dot_general(a, b, (contract, ((), ())), preferred_element_type=F32)


def spread_matrix(count):
    out = np.zeros((count * SIDE, count * SIDE // 2), np.float32)
    for a in range(count):
        for i in range(SIDE):
            out[a * SIDE + i, count * (i // 2) + a] = 1.0
    return out


def double_matrix():
    eye = huber_delta * np.eye(SIDE, dtype=np.float32)
    return np.kron(np.eye(2, dtype=np.float32), np.concatenate([eye, eye], 1))


def parity_mask(rows):
    row = lax.broadcasted_iota(jnp.int32, (rows, 128), 0)
    lane = lax.broadcasted_iota(jnp.int32, (rows, 128), 1)
    return (row & 1) == (lane >> 6)


def spread_pair(both, mask):
    col = jnp.where(mask, both[:, :128], 0.0).astype(BF16)
    col = col + pltpu.roll(col, 64, 1)
    row = jnp.where(mask, both[:, 128:], 0.0).astype(BF16)
    return col, row


def reproject_kernel(x_ref, col_ref, row_ref, spread_ref, out_ref, scratch):
    mask = parity_mask(256)
    spread = spread_ref[...]
    group = range(4)
    wide = [jnp.concatenate([x_ref[s], col_ref[s], row_ref[s]], 1) for s in group]
    wide = [dot(spread, w) for w in wide]
    planes = [jnp.where(mask, w[:, :128], 0.0).astype(BF16) for w in wide]
    pairs = [spread_pair(w[:, 128:], mask) for w in wide]
    halves = [dot(planes[s], pairs[s][0], ((1,), (1,))).astype(BF16) for s in group]
    for s in group:
        for k in range(4):
            lanes = slice(k * SIDE, (k + 1) * SIDE)
            part = [halves[s][c * SIDE : (c + 1) * SIDE, lanes] for c in range(4)]
            part = jnp.concatenate(part, 1)
            part = jnp.concatenate([part, part], 0)
            moved = dot(pairs[s][1][k * SIDE : (k + 1) * SIDE], part)
            for v in range(2):
                scratch[v, pl.ds(4 * k + s, SIDE, stride=16), :] = moved[:, v * 128 : (v + 1) * 128]
    for v in range(2):
        out_ref[:, :, v * 128 : (v + 1) * 128] = scratch[v].reshape(SIDE, 16, 128).astype(BF16)


def weight_kernel(place_ref, w_ref, id_ref, col_ref, row_ref, spread_ref, spread1_ref, *rest):
    outs, scratch = rest[:-1], rest[-1]
    mask = parity_mask(256)
    mask1 = parity_mask(SIDE)
    spread = spread_ref[...]
    spread1 = spread1_ref[...]
    group = range(4)
    planes = [jnp.where(mask1, dot(spread1, w_ref[s]), 0.0).astype(BF16) for s in group]
    wide = [dot(spread, jnp.concatenate([col_ref[s], row_ref[s]], 1)) for s in group]
    pairs = [spread_pair(x, mask) for x in wide]
    halves = [dot(planes[s], pairs[s][0], ((1,), (1,))) for s in group]
    for s in group:
        parts = []
        for k in range(4):
            part = halves[s][:, k * SIDE : (k + 1) * SIDE].astype(BF16)
            part = jnp.concatenate([part, part], 0)
            parts.append(dot(pairs[s][1][k * SIDE : (k + 1) * SIDE], part))
        for v in range(2):
            pair = jnp.concatenate(parts[2 * v : 2 * v + 2], 1)
            scratch[v, pl.ds(s, SIDE, stride=4), :] = pair
    ids = jnp.broadcast_to(id_ref[...].astype(BF16)[None], (8, 4, 128))
    for turn, out_ref in enumerate(outs):
        z = (place_ref[1] + turn) % 8
        for y in range(4):
            for v in range(2):
                line = scratch[v, pl.ds(pl.multiple_of(64 * y + 8 * z, 8), 8), :]
                out_ref[2 * y : 2 * y + 2, v] = line.reshape(2, 4, 128).astype(BF16)
        out_ref[:, 2] = ids


def stack_kernel(place_ref, *rest):
    parts, out_ref, ids = rest[:8], rest[8], rest[9]
    for turn, part in enumerate(parts):
        z = (place_ref[1] + 8 - turn) % 8
        for b in range(4):
            for v in range(2):
                out_ref[:, b, pl.ds(8 * v + z, 1)] = part[:, v : v + 1]
        ids[pl.ds(z, 1)] = jnp.broadcast_to(part[0, 2].astype(F32)[:1][None], (1, 8, 128))
    lines = jnp.concatenate([ids[z, :1] for z in range(8)], 0)
    lines = jnp.broadcast_to(lines.reshape(1, 2, 4, 128), (8, 2, 4, 128)).astype(BF16)
    for b in range(4):
        out_ref[:, b, 16:18] = lines


def after_kernel(x_ref, first_ref, out_ref):
    pass


def cloud_kernel(x0, x1, x2, x3, factor_ref, w_in_ref, w_hidden_ref, w_out_ref, out_ref):
    def silu_of_twice(u):
        return (u + u * jnp.tanh(u)).astype(BF16)

    scene, width = pl.program_id(0), factor_ref.shape[2]
    lanes = pl.ds(pl.multiple_of(pl.program_id(1) * width, width), width)
    x = jnp.concatenate([x_ref[scene, :, lanes] for x_ref in (x0, x1, x2, x3)], 0)
    hidden = silu_of_twice(dot(w_in_ref[...], x))
    for layer in range(2):
        hidden = silu_of_twice(dot(w_hidden_ref[layer], hidden))
    logits = dot(w_out_ref[...], hidden)[:1]
    weight = factor_ref[0] / (1.0 + jnp.exp(logits))
    lines = [weight[:, i * 128 : (i + 1) * 128] for i in range(weight.shape[1] // 128)]
    out_ref[0] = jnp.concatenate(lines, 0).astype(BF16)


def merge_kernel(y_in, w_ref, double_ref, out_ref, y_ref, pick, pick_t, weight, arrival):
    fetch = pltpu.make_async_copy(y_in, y_ref, arrival)
    fetch.start()
    entries = y_ref.shape[0]
    chunk = 512
    lane = lax.broadcasted_iota(jnp.int32, (1, 128), 1)
    tile = (lax.broadcasted_iota(jnp.int32, (128, 128), 0) & 63).astype(F32)
    ids = w_ref[:, 0, 16:18].astype(F32).reshape(8, 8, 128)
    turned = pltpu.roll(ids, 64, 2)
    for i in range(entries // 128):
        span = slice(i * 128, (i + 1) * 128)
        y, z = i // 8, i % 8
        pair = jnp.where(lane < 64, ids[2 * y, z : z + 1], turned[2 * y + 1, z : z + 1])
        hit = jnp.where(pair == tile, 1.0, 0.0)
        pick[:, span] = hit[:SIDE].astype(BF16)
        pick_t[span, :] = hit.T.astype(BF16)
    for b in range(4):
        for v in range(2):
            w = w_ref[:, b, 8 * v : 8 * v + 8].reshape(entries // 16, 128)
            w = dot(w, double_ref[...])
            for half in range(2):
                first = 16 * b + 8 * v + 4 * half
                part = w[:, half * 128 : (half + 1) * 128].reshape(4, 2, 8, 4, 128)
                for y in range(4):
                    for c in range(2):
                        weight[y, :, c, first : first + 4, :] = part[y, c]
    fetch.wait()

    def totals(estimate):
        top = bottom = 0.0
        if estimate is not None:
            high = estimate.astype(BF16)
            low = (estimate - high.astype(F32)).astype(BF16)
            stacked = jnp.concatenate([high, low], 0)
        spans = [slice(i * chunk, (i + 1) * chunk) for i in range(entries // chunk)]

        def expected(span):
            return None if estimate is None else dot(pick_t[span, :], stacked)

        ahead = expected(spans[0])
        for i, span in enumerate(spans):
            here, ahead = ahead, expected(spans[i + 1]) if i + 1 < len(spans) else None
            w = weight[i // 2, 4 * (i % 2) : 4 * (i % 2) + 4].reshape(chunk, 128)
            y = y_ref[span, :]
            h = jnp.concatenate([w, w], 1)
            if estimate is not None:
                h = h / jnp.maximum(jnp.abs(y.astype(F32) - here), huber_delta)
            h = h.astype(BF16)
            picked = pick[:, span]
            top = top + dot(picked, h * y)
            bottom = bottom + dot(picked, h)
        prior = prior_weight if estimate is not None else prior_weight * huber_delta
        return top / (bottom + prior)

    estimate = lax.fori_loop(0, HUBER_ITERS, lambda _, e: totals(e), totals(None))

    lane = lax.broadcasted_iota(jnp.int32, (SIDE, 128), 1)
    for v in range(2):
        own = estimate[:, v * 128 : (v + 1) * 128]
        turned = pltpu.roll(own, 64, 1)
        for odd in range(2):
            first, second = (turned, own) if odd else (own, turned)
            after = pltpu.roll(second, SIDE - 1, 0)
            before = pltpu.roll(second, 1, 0)
            out_ref[:, 2 * v + odd, :] = jnp.where(
                lane < 64, first, jnp.where(lane < 96, after, before)
            )


def smooth_kernel(tile_ref, g_ref, out_ref, scratch):
    first = tile_ref[0] == 0
    last = tile_ref[0] == tile_ref[1] - 1
    lane = lax.broadcasted_iota(jnp.int32, (SIDE, 128), 1)
    row = lax.broadcasted_iota(jnp.int32, (SIDE, 128), 0)
    closed = ((lane == 127) & first) | ((lane == SIDE - 1) & last)
    bottom = row == SIDE - 1

    def flux(d):
        return d / (1.0 + d * d)

    for c in range(4):
        g = g_ref[:, c, :]
        for repeat in range(SMOOTH):
            across = jnp.where(closed, 0.0, flux(pltpu.roll(g, 127, 1) - g))
            down = jnp.where(bottom, 0.0, flux(pltpu.roll(g, SIDE - 1, 0) - g))
            g = g + smooth_rate * (
                across - pltpu.roll(across, 1, 1) + (down - pltpu.roll(down, 1, 0))
            )
        scratch[c] = g
        even = scratch[c, pl.ds(0, SIDE // 2, stride=2), :]
        odd = scratch[c, pl.ds(1, SIDE // 2, stride=2), :]
        out_ref[:, c, :] = jnp.where(lane[: SIDE // 2] < SIDE, even, pltpu.roll(odd, SIDE, 1))


def two_rows_per_line(x):
    scenes, planes, _ = x.shape
    x = x.reshape(scenes, planes, SIDE // 2, 128)
    return x.transpose(0, 2, 1, 3).reshape(scenes, planes * SIDE // 2, 128)


def keep(x):
    return pltpu.with_memory_space_constraint(x, pltpu.VMEM)


def whole(shape):
    return pl.BlockSpec(shape, lambda *_: (0,) * len(shape))


def per_device(
    granules,
    valid_rows,
    scene_order,
    intersections,
    row_resample,
    col_resample,
    w_in,
    w_hidden,
    w_out,
):
    scenes, bands, pixels = granules.shape
    tiles = lax.axis_size("tile")
    groups = lax.axis_size("band")
    share = scenes // groups
    spread = jnp.asarray(spread_matrix(4), BF16)
    spread1 = jnp.asarray(spread_matrix(1), BF16)

    in_vmem = pl.BlockSpec(memory_space=pltpu.VMEM)
    cols = two_rows_per_line(col_resample)
    rows = two_rows_per_line(row_resample)
    scene_block = pl.BlockSpec((4, 128, 128), lambda i: (i, 0, 0))
    moved = pl.pallas_call(
        reproject_kernel,
        grid=(4,),
        in_specs=[scene_block, scene_block, scene_block, whole((256, 128))],
        out_specs=pl.BlockSpec((SIDE, 16, 256), lambda i: (0, i, 0)),
        out_shape=jax.ShapeDtypeStruct((SIDE, 64, 256), BF16),
        scratch_shapes=[pltpu.VMEM((2, SIDE * 16, 128), F32)],
        name="reproject",
    )(two_rows_per_line(granules), cols, rows, spread)
    moved, granules = lax.optimization_barrier((moved, granules))
    values = lax.all_to_all(moved, "tile", split_axis=0, concat_axis=0)

    band = lax.axis_index("band")
    by_group = granules.reshape(groups, share, bands, pixels)
    w_in = w_in.reshape(groups, bands, -1)
    layers, w_rows = [], []
    for turn in range(groups):
        part = lax.dynamic_index_in_dim(by_group, (band + turn) % groups, 0, keepdims=False)
        if turn:
            part = lax.ppermute(part, "band", [(i, (i + turn) % groups) for i in range(groups)])
        layers.append(part)
        w_rows.append(lax.dynamic_index_in_dim(w_in, (band - turn) % groups, 0, keepdims=False))
    w_in = jnp.concatenate(w_rows, 0)

    first_scene = band * share
    recency = jnp.exp(1.4 * scene_order.astype(F32) / (scenes * tiles) - 0.7)
    factor = valid_rows.astype(F32) * recency[:, None]
    factor = lax.dynamic_slice_in_dim(factor, first_scene, share, 0)
    factor = jnp.broadcast_to(factor[:, :, None], (share, SIDE, SIDE)).reshape(share, 1, pixels)
    half = jnp.asarray(0.5, BF16)
    width = 2048
    weights = pl.pallas_call(
        cloud_kernel,
        grid=(share, pixels // width),
        in_specs=[in_vmem] * groups
        + [
            pl.BlockSpec((1, 1, width), lambda s, i: (s, 0, i)),
            whole((256, 16)),
            whole((2, 256, 256)),
            whole((8, 256)),
        ],
        out_specs=pl.BlockSpec((1, width // 128, 128), lambda s, i: (s, i, 0)),
        out_shape=jax.ShapeDtypeStruct((share, SIDE // 2, 128), BF16),
        cost_estimate=pl.CostEstimate(flops=12 * 10**9, transcendentals=0, bytes_accessed=10**6),
        name="cloud",
    )(
        *map(keep, layers),
        factor,
        w_in.T * half,
        w_hidden.transpose(0, 2, 1) * half,
        jnp.broadcast_to(w_out[None, :], (8, 256)),
    )
    ids = intersections.reshape(groups, share, 4).transpose(0, 2, 1).reshape(1, scenes * 4)
    ids = jnp.broadcast_to(jnp.pad(ids, ((0, 0), (0, 128 - scenes * 4))).astype(F32), (4, 128))
    tile = lax.axis_index("tile")
    place = jnp.stack([band, (tile // 2) % 8]).astype(jnp.int32)
    mine = pl.BlockSpec((4, 128, 128), lambda i, place: (place[0], 0, 0))
    pieces = pl.pallas_call(
        weight_kernel,
        grid_spec=pltpu.PrefetchScalarGridSpec(
            num_scalar_prefetch=1,
            grid=(1,),
            in_specs=[
                whole((share, SIDE // 2, 128)),
                whole((4, 128)),
                mine,
                mine,
                whole((256, 128)),
                whole((SIDE, SIDE // 2)),
            ],
            out_specs=[whole((8, 3, share, 128))] * 8,
            scratch_shapes=[pltpu.VMEM((2, SIDE * share, 128), F32)],
        ),
        out_shape=[jax.ShapeDtypeStruct((8, 3, share, 128), BF16)] * 8,
        cost_estimate=pl.CostEstimate(flops=3 * 10**9, transcendentals=0, bytes_accessed=10**6),
        name="reproject_weights",
    )(place, weights, ids, cols, rows, spread, spread1)
    along_z = [
        [(t, t // 16 * 16 + (t // 2 + turn) % 8 * 2 + t % 2) for t in range(tiles)] for turn in range(8)
    ]
    pieces = [pieces[0]] + [lax.ppermute(pieces[t], "tile", along_z[t]) for t in range(1, 8)]
    moved_weights = pl.pallas_call(
        stack_kernel,
        in_specs=[pl.BlockSpec(memory_space=pltpu.SMEM)] + [in_vmem] * 8,
        out_shape=jax.ShapeDtypeStruct((8, groups, 18, share, 128), BF16),
        scratch_shapes=[pltpu.VMEM((8, 8, 128), F32)],
        name="stack",
    )(place, *map(keep, pieces))
    anywhere = pl.BlockSpec(memory_space=pl.ANY)
    moved_weights = pl.pallas_call(
        after_kernel,
        in_specs=[anywhere, anywhere],
        out_specs=anywhere,
        out_shape=jax.ShapeDtypeStruct(moved_weights.shape, BF16),
        input_output_aliases={0: 0},
        name="after",
    )(moved_weights, keep(values))
    same_z = [
        [(16 * y + 2 * z + c) * groups + b for y in range(4) for c in range(2) for b in range(groups)]
        for z in range(8)
    ]
    moved_weights = lax.all_to_all(
        moved_weights.reshape(8 * groups, 18, share, 128),
        ("tile", "band"),
        split_axis=0,
        concat_axis=0,
        axis_index_groups=same_z,
    ).reshape(8, groups, 18, share, 128)

    entries = tiles * scenes * 4
    estimate = pl.pallas_call(
        merge_kernel,
        in_specs=[anywhere, in_vmem, in_vmem],
        out_shape=jax.ShapeDtypeStruct((tiles, 4, 128), F32),
        scratch_shapes=[
            pltpu.VMEM((entries, 256), BF16),
            pltpu.VMEM((SIDE, entries), BF16),
            pltpu.VMEM((entries, 128), BF16),
            pltpu.VMEM((4, 8, 2, SIDE, 128), F32),
            pltpu.SemaphoreType.DMA,
        ],
        name="merge",
    )(values.reshape(entries, 256), keep(moved_weights), jnp.asarray(double_matrix(), BF16))
    field = lax.all_to_all(estimate, "tile", split_axis=0, concat_axis=0)

    place = jnp.stack([tile, tiles]).astype(jnp.int32)
    out = pl.pallas_call(
        smooth_kernel,
        in_specs=[pl.BlockSpec(memory_space=pltpu.SMEM), in_vmem],
        out_shape=jax.ShapeDtypeStruct((SIDE // 2, 4, 128), F32),
        scratch_shapes=[pltpu.VMEM((4, SIDE, 128), F32)],
        name="smooth",
    )(place, keep(field))
    return out.transpose(1, 0, 2).reshape(4, pixels)


def solution(mesh):
    return jax.shard_map(
        per_device,
        mesh=mesh,
        in_specs=(
            P("tile", "band", None),
            P("tile", None),
            P("tile"),
            P("tile", None),
            P("tile", None, None),
            P("tile", None, None),
            P(),
            P(),
            P(),
        ),
        out_specs=P("band", "tile"),
        check_vma=False,
    )
```

```python
import jax
import jax.numpy as jnp
import numpy as np
from jax import lax
from jax.experimental import pallas as pl
from jax.experimental.pallas import tpu as pltpu
from jax.sharding import PartitionSpec as P

HUBER_ITERS = 4
SMOOTH = 2

prior_weight = 0.25
huber_delta = 0.5
smooth_rate = 0.2

F32 = jnp.float32
BF16 = jnp.bfloat16
SIDE = 64


def dot(a, b, contract=((1,), (0,))):
    return lax.dot_general(a, b, (contract, ((), ())), preferred_element_type=F32)


def spread_matrix(count):
    out = np.zeros((count * SIDE, count * SIDE // 2), np.float32)
    for a in range(count):
        for i in range(SIDE):
            out[a * SIDE + i, count * (i // 2) + a] = 1.0
    return out


def double_matrix():
    eye = huber_delta * np.eye(SIDE, dtype=np.float32)
    return np.kron(np.eye(2, dtype=np.float32), np.concatenate([eye, eye], 1))


def parity_mask(rows):
    row = lax.broadcasted_iota(jnp.int32, (rows, 128), 0)
    lane = lax.broadcasted_iota(jnp.int32, (rows, 128), 1)
    return (row & 1) == (lane >> 6)


def spread_pair(both, mask):
    col = jnp.where(mask, both[:, :128], 0.0).astype(BF16)
    col = col + pltpu.roll(col, 64, 1)
    row = jnp.where(mask, both[:, 128:], 0.0).astype(BF16)
    return col, row


def reproject_kernel(x_ref, col_ref, row_ref, spread_ref, out_ref, scratch):
    mask = parity_mask(256)
    spread = spread_ref[...]
    group = range(4)
    wide = [jnp.concatenate([x_ref[s], col_ref[s], row_ref[s]], 1) for s in group]
    wide = [dot(spread, w) for w in wide]
    planes = [jnp.where(mask, w[:, :128], 0.0).astype(BF16) for w in wide]
    pairs = [spread_pair(w[:, 128:], mask) for w in wide]
    halves = [dot(planes[s], pairs[s][0], ((1,), (1,))).astype(BF16) for s in group]
    for s in group:
        for k in range(4):
            lanes = slice(k * SIDE, (k + 1) * SIDE)
            part = [halves[s][c * SIDE : (c + 1) * SIDE, lanes] for c in range(4)]
            part = jnp.concatenate(part, 1)
            part = jnp.concatenate([part, part], 0)
            moved = dot(pairs[s][1][k * SIDE : (k + 1) * SIDE], part)
            for v in range(2):
                scratch[v, pl.ds(4 * k + s, SIDE, stride=16), :] = moved[:, v * 128 : (v + 1) * 128]
    for v in range(2):
        out_ref[:, :, v * 128 : (v + 1) * 128] = scratch[v].reshape(SIDE, 16, 128).astype(BF16)


def weight_kernel(place_ref, w_ref, id_ref, col_ref, row_ref, spread_ref, spread1_ref, *rest):
    outs, scratch = rest[:-1], rest[-1]
    mask = parity_mask(256)
    mask1 = parity_mask(SIDE)
    spread = spread_ref[...]
    spread1 = spread1_ref[...]
    group = range(4)
    planes = [jnp.where(mask1, dot(spread1, w_ref[s]), 0.0).astype(BF16) for s in group]
    wide = [dot(spread, jnp.concatenate([col_ref[s], row_ref[s]], 1)) for s in group]
    pairs = [spread_pair(x, mask) for x in wide]
    halves = [dot(planes[s], pairs[s][0], ((1,), (1,))) for s in group]
    for s in group:
        parts = []
        for k in range(4):
            part = halves[s][:, k * SIDE : (k + 1) * SIDE].astype(BF16)
            part = jnp.concatenate([part, part], 0)
            parts.append(dot(pairs[s][1][k * SIDE : (k + 1) * SIDE], part))
        for v in range(2):
            pair = jnp.concatenate(parts[2 * v : 2 * v + 2], 1)
            scratch[v, pl.ds(s, SIDE, stride=4), :] = pair
    ids = jnp.broadcast_to(id_ref[...].astype(BF16)[None], (16, 4, 128))
    for turn, out_ref in enumerate(outs):
        pair = (place_ref[1] + turn) % 4
        for y in range(4):
            for v in range(2):
                line = scratch[v, pl.ds(pl.multiple_of(64 * y + 16 * pair, 16), 16), :]
                out_ref[4 * y : 4 * y + 4, v] = line.reshape(4, 4, 128).astype(BF16)
        out_ref[:, 2] = ids


def after_kernel(x_ref, first_ref, out_ref):
    pass


def stack_kernel(place_ref, p0, p1, p2, p3, out_ref, ids):
    for turn, part in enumerate((p0, p1, p2, p3)):
        pair = (place_ref[1] + 4 - turn) % 4
        for b in range(4):
            for v in range(2):
                out_ref[:, b, pl.ds(4 * v + pair, 1)] = part[:, v : v + 1]
        ids[pl.ds(pair, 1)] = jnp.broadcast_to(part[0, 2].astype(F32)[:1][None], (1, 8, 128))
    lines = jnp.concatenate([ids[z, :1] for z in range(4)], 0)
    lines = jnp.broadcast_to(lines[None], (16, 4, 128)).astype(BF16)
    for b in range(4):
        out_ref[:, b, 8] = lines


def cloud_kernel(x0, x1, x2, x3, factor_ref, w_in_ref, w_hidden_ref, w_out_ref, out_ref):
    def silu_of_twice(u):
        return (u + u * jnp.tanh(u)).astype(BF16)

    scene, width = pl.program_id(0), factor_ref.shape[2]
    lanes = pl.ds(pl.multiple_of(pl.program_id(1) * width, width), width)
    x = jnp.concatenate([x_ref[scene, :, lanes] for x_ref in (x0, x1, x2, x3)], 0)
    hidden = silu_of_twice(dot(w_in_ref[...], x))
    for layer in range(2):
        hidden = silu_of_twice(dot(w_hidden_ref[layer], hidden))
    logits = dot(w_out_ref[...], hidden)[:1]
    weight = factor_ref[0] / (1.0 + jnp.exp(logits))
    lines = [weight[:, i * 128 : (i + 1) * 128] for i in range(weight.shape[1] // 128)]
    out_ref[0] = jnp.concatenate(lines, 0).astype(BF16)


def merge_kernel(y_in, w_ref, double_ref, out_ref, y_ref, pick, pick_t, weight, arrival):
    fetch = pltpu.make_async_copy(y_in, y_ref, arrival)
    fetch.start()
    entries = y_ref.shape[0]
    chunk = 512
    lane = lax.broadcasted_iota(jnp.int32, (1, 128), 1)
    tile = (lax.broadcasted_iota(jnp.int32, (128, 128), 0) & 63).astype(F32)
    ids = w_ref[:, 0, 8].astype(F32)
    turned = pltpu.roll(ids, 64, 2)
    for i in range(entries // 128):
        span = slice(i * 128, (i + 1) * 128)
        at, z = i // 8 * 4 + i % 2 * 2, i % 8 // 2
        pair = jnp.where(lane < 64, ids[at, z : z + 1], turned[at + 1, z : z + 1])
        hit = jnp.where(pair == tile, 1.0, 0.0)
        pick[:, span] = hit[:SIDE].astype(BF16)
        pick_t[span, :] = hit.T.astype(BF16)
    for b in range(4):
        for v in range(2):
            w = w_ref[:, b, 4 * v : 4 * v + 4].reshape(entries // 16, 128)
            w = dot(w, double_ref[...])
            for half in range(2):
                first = 16 * b + 8 * v + 4 * half
                part = w[:, half * 128 : (half + 1) * 128].reshape(4, 4, 4, 4, 128)
                for y in range(4):
                    for low in range(4):
                        weight[y, :, low, first : first + 4, :] = part[y, low]
    fetch.wait()

    def totals(estimate):
        top = bottom = 0.0
        if estimate is not None:
            high = estimate.astype(BF16)
            low = (estimate - high.astype(F32)).astype(BF16)
            stacked = jnp.concatenate([high, low], 0)
        spans = [slice(i * chunk, (i + 1) * chunk) for i in range(entries // chunk)]

        def expected(span):
            return None if estimate is None else dot(pick_t[span, :], stacked)

        ahead = expected(spans[0])
        for i, span in enumerate(spans):
            here, ahead = ahead, expected(spans[i + 1]) if i + 1 < len(spans) else None
            w = weight[i // 2, 2 * (i % 2) : 2 * (i % 2) + 2].reshape(chunk, 128)
            y = y_ref[span, :]
            h = jnp.concatenate([w, w], 1)
            if estimate is not None:
                h = h / jnp.maximum(jnp.abs(y.astype(F32) - here), huber_delta)
            h = h.astype(BF16)
            picked = pick[:, span]
            top = top + dot(picked, h * y)
            bottom = bottom + dot(picked, h)
        prior = prior_weight if estimate is not None else prior_weight * huber_delta
        return top / (bottom + prior)

    estimate = lax.fori_loop(0, HUBER_ITERS, lambda _, e: totals(e), totals(None))

    lane = lax.broadcasted_iota(jnp.int32, (SIDE, 128), 1)
    for v in range(2):
        own = estimate[:, v * 128 : (v + 1) * 128]
        turned = pltpu.roll(own, 64, 1)
        for odd in range(2):
            first, second = (turned, own) if odd else (own, turned)
            after = pltpu.roll(second, SIDE - 1, 0)
            before = pltpu.roll(second, 1, 0)
            out_ref[:, 2 * v + odd, :] = jnp.where(
                lane < 64, first, jnp.where(lane < 96, after, before)
            )


def smooth_kernel(tile_ref, g_ref, out_ref, scratch):
    first = tile_ref[0] == 0
    last = tile_ref[0] == tile_ref[1] - 1
    lane = lax.broadcasted_iota(jnp.int32, (SIDE, 128), 1)
    row = lax.broadcasted_iota(jnp.int32, (SIDE, 128), 0)
    closed = ((lane == 127) & first) | ((lane == SIDE - 1) & last)
    bottom = row == SIDE - 1

    def flux(d):
        return d / (1.0 + d * d)

    for c in range(4):
        g = g_ref[:, c, :]
        for repeat in range(SMOOTH):
            across = jnp.where(closed, 0.0, flux(pltpu.roll(g, 127, 1) - g))
            down = jnp.where(bottom, 0.0, flux(pltpu.roll(g, SIDE - 1, 0) - g))
            g = g + smooth_rate * (
                across - pltpu.roll(across, 1, 1) + (down - pltpu.roll(down, 1, 0))
            )
        scratch[c] = g
        even = scratch[c, pl.ds(0, SIDE // 2, stride=2), :]
        odd = scratch[c, pl.ds(1, SIDE // 2, stride=2), :]
        out_ref[:, c, :] = jnp.where(lane[: SIDE // 2] < SIDE, even, pltpu.roll(odd, SIDE, 1))


def two_rows_per_line(x):
    scenes, planes, _ = x.shape
    x = x.reshape(scenes, planes, SIDE // 2, 128)
    return x.transpose(0, 2, 1, 3).reshape(scenes, planes * SIDE // 2, 128)


def keep(x):
    return pltpu.with_memory_space_constraint(x, pltpu.VMEM)


def whole(shape):
    return pl.BlockSpec(shape, lambda *_: (0,) * len(shape))


def per_device(
    granules,
    valid_rows,
    scene_order,
    intersections,
    row_resample,
    col_resample,
    w_in,
    w_hidden,
    w_out,
):
    scenes, bands, pixels = granules.shape
    tiles = lax.axis_size("tile")
    groups = lax.axis_size("band")
    share = scenes // groups
    spread = jnp.asarray(spread_matrix(4), BF16)
    spread1 = jnp.asarray(spread_matrix(1), BF16)

    in_vmem = pl.BlockSpec(memory_space=pltpu.VMEM)
    cols = two_rows_per_line(col_resample)
    rows = two_rows_per_line(row_resample)
    scene_block = pl.BlockSpec((4, 128, 128), lambda i: (i, 0, 0))
    moved = pl.pallas_call(
        reproject_kernel,
        grid=(4,),
        in_specs=[scene_block, scene_block, scene_block, whole((256, 128))],
        out_specs=pl.BlockSpec((SIDE, 16, 256), lambda i: (0, i, 0)),
        out_shape=jax.ShapeDtypeStruct((SIDE, 64, 256), BF16),
        scratch_shapes=[pltpu.VMEM((2, SIDE * 16, 128), F32)],
        name="reproject",
    )(two_rows_per_line(granules), cols, rows, spread)
    moved, granules = lax.optimization_barrier((moved, granules))
    values = lax.all_to_all(moved, "tile", split_axis=0, concat_axis=0)

    band = lax.axis_index("band")
    by_group = granules.reshape(groups, share, bands, pixels)
    w_in = w_in.reshape(groups, bands, -1)
    layers, w_rows = [], []
    for turn in range(groups):
        part = lax.dynamic_index_in_dim(by_group, (band + turn) % groups, 0, keepdims=False)
        if turn:
            part = lax.ppermute(part, "band", [(i, (i + turn) % groups) for i in range(groups)])
        layers.append(part)
        w_rows.append(lax.dynamic_index_in_dim(w_in, (band - turn) % groups, 0, keepdims=False))
    w_in = jnp.concatenate(w_rows, 0)

    first_scene = band * share
    recency = jnp.exp(1.4 * scene_order.astype(F32) / (scenes * tiles) - 0.7)
    factor = valid_rows.astype(F32) * recency[:, None]
    factor = lax.dynamic_slice_in_dim(factor, first_scene, share, 0)
    factor = jnp.broadcast_to(factor[:, :, None], (share, SIDE, SIDE)).reshape(share, 1, pixels)
    half = jnp.asarray(0.5, BF16)
    width = 2048
    weights = pl.pallas_call(
        cloud_kernel,
        grid=(share, pixels // width),
        in_specs=[in_vmem] * groups
        + [
            pl.BlockSpec((1, 1, width), lambda s, i: (s, 0, i)),
            whole((256, 16)),
            whole((2, 256, 256)),
            whole((8, 256)),
        ],
        out_specs=pl.BlockSpec((1, width // 128, 128), lambda s, i: (s, i, 0)),
        out_shape=jax.ShapeDtypeStruct((share, SIDE // 2, 128), BF16),
        cost_estimate=pl.CostEstimate(flops=12 * 10**9, transcendentals=0, bytes_accessed=10**6),
        name="cloud",
    )(
        *map(keep, layers),
        factor,
        w_in.T * half,
        w_hidden.transpose(0, 2, 1) * half,
        jnp.broadcast_to(w_out[None, :], (8, 256)),
    )
    ids = intersections.reshape(groups, share, 4).transpose(0, 2, 1).reshape(1, scenes * 4)
    ids = jnp.broadcast_to(jnp.pad(ids, ((0, 0), (0, 128 - scenes * 4))).astype(F32), (4, 128))
    tile = lax.axis_index("tile")
    place = jnp.stack([band, (tile // 4) % 4]).astype(jnp.int32)
    mine = pl.BlockSpec((4, 128, 128), lambda i, place: (place[0], 0, 0))
    pieces = pl.pallas_call(
        weight_kernel,
        grid_spec=pltpu.PrefetchScalarGridSpec(
            num_scalar_prefetch=1,
            grid=(1,),
            in_specs=[
                whole((share, SIDE // 2, 128)),
                whole((4, 128)),
                mine,
                mine,
                whole((256, 128)),
                whole((SIDE, SIDE // 2)),
            ],
            out_specs=[whole((16, 3, share, 128))] * 4,
            scratch_shapes=[pltpu.VMEM((2, SIDE * share, 128), F32)],
        ),
        out_shape=[jax.ShapeDtypeStruct((16, 3, share, 128), BF16)] * 4,
        cost_estimate=pl.CostEstimate(flops=3 * 10**9, transcendentals=0, bytes_accessed=10**6),
        name="reproject_weights",
    )(place, weights, ids, cols, rows, spread, spread1)
    along_z = [
        [(t, t // 16 * 16 + (t // 4 + turn) % 4 * 4 + t % 4) for t in range(tiles)] for turn in range(4)
    ]
    pieces = [pieces[0]] + [keep(lax.ppermute(pieces[t], "tile", along_z[t])) for t in range(1, 4)]
    anywhere = pl.BlockSpec(memory_space=pl.ANY)
    moved_weights = pl.pallas_call(
        stack_kernel,
        in_specs=[pl.BlockSpec(memory_space=pltpu.SMEM)] + [in_vmem] * 4,
        out_shape=jax.ShapeDtypeStruct((16, groups, 9, share, 128), BF16),
        scratch_shapes=[pltpu.VMEM((4, 8, 128), F32)],
        name="stack",
    )(place, *pieces)
    moved_weights = pl.pallas_call(
        after_kernel,
        in_specs=[anywhere, anywhere],
        out_specs=anywhere,
        out_shape=jax.ShapeDtypeStruct(moved_weights.shape, BF16),
        input_output_aliases={0: 0},
        name="after",
    )(moved_weights, keep(values))
    same_pair = [
        [(16 * y + 4 * z + low) * groups + b for y in range(4) for low in range(4) for b in range(groups)]
        for z in range(4)
    ]
    moved_weights = lax.all_to_all(
        moved_weights.reshape(16 * groups, 9, share, 128),
        ("tile", "band"),
        split_axis=0,
        concat_axis=0,
        axis_index_groups=same_pair,
    ).reshape(16, groups, 9, share, 128)

    entries = tiles * scenes * 4
    estimate = pl.pallas_call(
        merge_kernel,
        in_specs=[anywhere, in_vmem, in_vmem],
        out_shape=jax.ShapeDtypeStruct((tiles, 4, 128), F32),
        scratch_shapes=[
            pltpu.VMEM((entries, 256), BF16),
            pltpu.VMEM((SIDE, entries), BF16),
            pltpu.VMEM((entries, 128), BF16),
            pltpu.VMEM((4, 4, 4, SIDE, 128), F32),
            pltpu.SemaphoreType.DMA,
        ],
        name="merge",
    )(values.reshape(entries, 256), keep(moved_weights), jnp.asarray(double_matrix(), BF16))
    field = lax.all_to_all(estimate, "tile", split_axis=0, concat_axis=0)

    place = jnp.stack([tile, tiles]).astype(jnp.int32)
    out = pl.pallas_call(
        smooth_kernel,
        in_specs=[pl.BlockSpec(memory_space=pltpu.SMEM), in_vmem],
        out_shape=jax.ShapeDtypeStruct((SIDE // 2, 4, 128), F32),
        scratch_shapes=[pltpu.VMEM((4, SIDE, 128), F32)],
        name="smooth",
    )(place, keep(field))
    return out.transpose(1, 0, 2).reshape(4, pixels)


def solution(mesh):
    return jax.shard_map(
        per_device,
        mesh=mesh,
        in_specs=(
            P("tile", "band", None),
            P("tile", None),
            P("tile"),
            P("tile", None),
            P("tile", None, None),
            P("tile", None, None),
            P(),
            P(),
            P(),
        ),
        out_specs=P("band", "tile"),
        check_vma=False,
    )
```

```python
import jax
import jax.numpy as jnp
import numpy as np
from jax import lax
from jax.experimental import pallas as pl
from jax.experimental.pallas import tpu as pltpu
from jax.sharding import PartitionSpec as P

HUBER_ITERS = 4
SMOOTH = 2

prior_weight = 0.25
huber_delta = 0.5
smooth_rate = 0.2

F32 = jnp.float32
BF16 = jnp.bfloat16
SIDE = 64


def dot(a, b, contract=((1,), (0,))):
    return lax.dot_general(a, b, (contract, ((), ())), preferred_element_type=F32)


def spread_matrix(count):
    out = np.zeros((count * SIDE, count * SIDE // 2), np.float32)
    for a in range(count):
        for i in range(SIDE):
            out[a * SIDE + i, count * (i // 2) + a] = 1.0
    return out


def double_matrix():
    eye = huber_delta * np.eye(SIDE, dtype=np.float32)
    return np.kron(np.eye(2, dtype=np.float32), np.concatenate([eye, eye], 1))


def parity_mask(rows):
    row = lax.broadcasted_iota(jnp.int32, (rows, 128), 0)
    lane = lax.broadcasted_iota(jnp.int32, (rows, 128), 1)
    return (row & 1) == (lane >> 6)


def spread_pair(both, mask):
    col = jnp.where(mask, both[:, :128], 0.0).astype(BF16)
    col = col + pltpu.roll(col, 64, 1)
    row = jnp.where(mask, both[:, 128:], 0.0).astype(BF16)
    return col, row


def reproject_kernel(x_ref, col_ref, row_ref, spread_ref, out_ref, scratch):
    mask = parity_mask(256)
    spread = spread_ref[...]
    group = range(8)
    wide = [jnp.concatenate([x_ref[s], col_ref[s], row_ref[s]], 1) for s in group]
    wide = [dot(spread, w) for w in wide]
    planes = [jnp.where(mask, w[:, :128], 0.0).astype(BF16) for w in wide]
    pairs = [spread_pair(w[:, 128:], mask) for w in wide]
    halves = [dot(planes[s], pairs[s][0], ((1,), (1,))).astype(BF16) for s in group]
    for s in group:
        for k in range(4):
            lanes = slice(k * SIDE, (k + 1) * SIDE)
            part = [halves[s][c * SIDE : (c + 1) * SIDE, lanes] for c in range(4)]
            part = jnp.concatenate(part, 1)
            part = jnp.concatenate([part, part], 0)
            moved = dot(pairs[s][1][k * SIDE : (k + 1) * SIDE], part)
            for v in range(2):
                at = pl.ds(4 * k + s % 4, SIDE, stride=16)
                scratch[s // 4, v, at, :] = moved[:, v * 128 : (v + 1) * 128]
    for g in range(2):
        for v in range(2):
            lines = scratch[g, v].reshape(SIDE, 16, 128).astype(BF16)
            out_ref[:, 16 * g : 16 * g + 16, v * 128 : (v + 1) * 128] = lines


def reproject_call(x, cols, rows, name):
    steps = x.shape[0] // 8
    scene_block = pl.BlockSpec((8, 128, 128), lambda i: (i, 0, 0))
    return pl.pallas_call(
        reproject_kernel,
        grid=(steps,),
        in_specs=[scene_block, scene_block, scene_block, whole((256, 128))],
        out_specs=pl.BlockSpec((SIDE, 32, 256), lambda i: (0, i, 0)),
        out_shape=jax.ShapeDtypeStruct((SIDE, 32 * steps, 256), BF16),
        scratch_shapes=[pltpu.VMEM((2, 2, SIDE * 16, 128), F32)],
        name=name,
    )(x, cols, rows, jnp.asarray(spread_matrix(4), BF16))


def weight_kernel(
    band_ref, w0, w1, w2, w3, id_ref, col_ref, row_ref, spread_ref, spread1_ref, out_ref, scratch
):
    turn = pl.program_id(0)
    place = 2 * ((band_ref[0] + 4 - turn) % 4)
    mask = parity_mask(256)
    mask1 = parity_mask(SIDE)
    spread = spread_ref[...]
    spread1 = spread1_ref[...]
    group = range(4)
    w = jnp.where(turn < 2, jnp.where(turn < 1, w0[...], w1[...]), jnp.where(turn < 3, w2[...], w3[...]))
    planes = [jnp.where(mask1, dot(spread1, w[s]), 0.0).astype(BF16) for s in group]
    wide = [dot(spread, jnp.concatenate([col_ref[s], row_ref[s]], 1)) for s in group]
    pairs = [spread_pair(x, mask) for x in wide]
    halves = [dot(planes[s], pairs[s][0], ((1,), (1,))) for s in group]
    for s in group:
        parts = []
        for k in range(4):
            part = halves[s][:, k * SIDE : (k + 1) * SIDE].astype(BF16)
            part = jnp.concatenate([part, part], 0)
            parts.append(dot(pairs[s][1][k * SIDE : (k + 1) * SIDE], part))
        for v in range(2):
            pair = jnp.concatenate(parts[2 * v : 2 * v + 2], 1)
            scratch[v, pl.ds(s, SIDE, stride=4), :] = pair
    for v in range(2):
        out_ref[:, place + v] = scratch[v].reshape(SIDE, 4, 128).astype(BF16)

    @pl.when(turn == 0)
    def _():
        out_ref[:, 8] = jnp.broadcast_to(id_ref[...].astype(BF16)[None], (SIDE, 4, 128))


def after_kernel(x_ref, first_ref, out_ref):
    pass


def cloud_kernel(x0, x1, x2, x3, factor_ref, w_in_ref, w_hidden_ref, w_out_ref, out_ref):
    def silu_of_twice(u):
        return (u + u * jnp.tanh(u)).astype(BF16)

    scene, width = pl.program_id(0), factor_ref.shape[2]
    lanes = pl.ds(pl.multiple_of(pl.program_id(1) * width, width), width)
    x = jnp.concatenate([x_ref[scene, :, lanes] for x_ref in (x0, x1, x2, x3)], 0)
    hidden = silu_of_twice(dot(w_in_ref[...], x))
    for layer in range(2):
        hidden = silu_of_twice(dot(w_hidden_ref[layer], hidden))
    logits = dot(w_out_ref[...], hidden)[:1]
    weight = factor_ref[0] / (1.0 + jnp.exp(logits))
    lines = [weight[:, i * 128 : (i + 1) * 128] for i in range(weight.shape[1] // 128)]
    out_ref[0] = jnp.concatenate(lines, 0).astype(BF16)


def merge_kernel(y_in, w_ref, double_ref, out_ref, y_ref, pick, pick_t, weight, arrival):
    fetch = pltpu.make_async_copy(y_in, y_ref, arrival)
    fetch.start()
    entries = y_ref.shape[0]
    chunk = 1024
    lane = lax.broadcasted_iota(jnp.int32, (1, 128), 1)
    tile = (lax.broadcasted_iota(jnp.int32, (128, 128), 0) & 63).astype(F32)
    ids = w_ref[:, 8].astype(F32)[:, 0, :]
    turned = pltpu.roll(ids, 64, 1)
    for i in range(entries // 128):
        span = slice(i * 128, (i + 1) * 128)
        pair = jnp.where(lane < 64, ids[2 * i : 2 * i + 1], turned[2 * i + 1 : 2 * i + 2])
        hit = jnp.where(pair == tile, 1.0, 0.0)
        pick[:, span] = hit[:SIDE].astype(BF16)
        pick_t[span, :] = hit.T.astype(BF16)
    for i in range(8):
        w = dot(w_ref[:, i].reshape(entries // 16, 128), double_ref[...])
        for half in range(2):
            first = 8 * i + 4 * half
            weight[:, first : first + 4, :] = w[:, half * 128 : (half + 1) * 128].reshape(
                entries // SIDE, 4, 128
            )
    fetch.wait()

    def totals(estimate):
        top = bottom = 0.0
        if estimate is not None:
            high = estimate.astype(BF16)
            low = (estimate - high.astype(F32)).astype(BF16)
            stacked = jnp.concatenate([high, low], 0)
        spans = [slice(i * chunk, (i + 1) * chunk) for i in range(entries // chunk)]

        def expected(span):
            return None if estimate is None else dot(pick_t[span, :], stacked)

        ahead = expected(spans[0])
        for i, span in enumerate(spans):
            here, ahead = ahead, expected(spans[i + 1]) if i + 1 < len(spans) else None
            w = weight[i * chunk // SIDE : (i + 1) * chunk // SIDE].reshape(chunk, 128)
            y = y_ref[span, :]
            h = jnp.concatenate([w, w], 1)
            if estimate is not None:
                h = h / jnp.maximum(jnp.abs(y.astype(F32) - here), huber_delta)
            h = h.astype(BF16)
            picked = pick[:, span]
            top = top + dot(picked, h * y)
            bottom = bottom + dot(picked, h)
        prior = prior_weight if estimate is not None else prior_weight * huber_delta
        return top / (bottom + prior)

    estimate = lax.fori_loop(0, HUBER_ITERS, lambda _, e: totals(e), totals(None))

    lane = lax.broadcasted_iota(jnp.int32, (SIDE, 128), 1)
    for v in range(2):
        own = estimate[:, v * 128 : (v + 1) * 128]
        turned = pltpu.roll(own, 64, 1)
        for odd in range(2):
            first, second = (turned, own) if odd else (own, turned)
            after = pltpu.roll(second, SIDE - 1, 0)
            before = pltpu.roll(second, 1, 0)
            out_ref[:, 2 * v + odd, :] = jnp.where(
                lane < 64, first, jnp.where(lane < 96, after, before)
            )


def smooth_kernel(tile_ref, g_ref, out_ref, scratch):
    first = tile_ref[0] == 0
    last = tile_ref[0] == tile_ref[1] - 1
    lane = lax.broadcasted_iota(jnp.int32, (SIDE, 128), 1)
    row = lax.broadcasted_iota(jnp.int32, (SIDE, 128), 0)
    closed = ((lane == 127) & first) | ((lane == SIDE - 1) & last)
    bottom = row == SIDE - 1

    def flux(d):
        return d / (1.0 + d * d)

    for c in range(4):
        g = g_ref[:, c, :]
        for repeat in range(SMOOTH):
            across = jnp.where(closed, 0.0, flux(pltpu.roll(g, 127, 1) - g))
            down = jnp.where(bottom, 0.0, flux(pltpu.roll(g, SIDE - 1, 0) - g))
            g = g + smooth_rate * (
                across - pltpu.roll(across, 1, 1) + (down - pltpu.roll(down, 1, 0))
            )
        scratch[c] = g
        even = scratch[c, pl.ds(0, SIDE // 2, stride=2), :]
        odd = scratch[c, pl.ds(1, SIDE // 2, stride=2), :]
        out_ref[:, c, :] = jnp.where(lane[: SIDE // 2] < SIDE, even, pltpu.roll(odd, SIDE, 1))


def two_rows_per_line(x):
    scenes, planes, _ = x.shape
    x = x.reshape(scenes, planes, SIDE // 2, 128)
    return x.transpose(0, 2, 1, 3).reshape(scenes, planes * SIDE // 2, 128)


def keep(x):
    return pltpu.with_memory_space_constraint(x, pltpu.VMEM)


def whole(shape):
    return pl.BlockSpec(shape, lambda *_: (0,) * len(shape))


def per_device(
    granules,
    valid_rows,
    scene_order,
    intersections,
    row_resample,
    col_resample,
    w_in,
    w_hidden,
    w_out,
):
    scenes, bands, pixels = granules.shape
    tiles = lax.axis_size("tile")
    groups = lax.axis_size("band")
    share = scenes // groups
    spread = jnp.asarray(spread_matrix(4), BF16)
    spread1 = jnp.asarray(spread_matrix(1), BF16)

    in_vmem = pl.BlockSpec(memory_space=pltpu.VMEM)
    cols = two_rows_per_line(col_resample)
    rows = two_rows_per_line(row_resample)
    moved = reproject_call(two_rows_per_line(granules), cols, rows, "reproject")
    moved, granules = lax.optimization_barrier((moved, granules))
    values = lax.all_to_all(moved, "tile", split_axis=0, concat_axis=0)

    band = lax.axis_index("band")
    by_group = granules.reshape(groups, share, bands, pixels)
    w_in = w_in.reshape(groups, bands, -1)
    layers, w_rows = [], []
    for turn in range(groups):
        part = lax.dynamic_index_in_dim(by_group, (band + turn) % groups, 0, keepdims=False)
        if turn:
            part = lax.ppermute(part, "band", [(i, (i + turn) % groups) for i in range(groups)])
        layers.append(part)
        w_rows.append(lax.dynamic_index_in_dim(w_in, (band - turn) % groups, 0, keepdims=False))
    w_in = jnp.concatenate(w_rows, 0)

    first_scene = band * share
    recency = jnp.exp(1.4 * scene_order.astype(F32) / (scenes * tiles) - 0.7)
    factor = valid_rows.astype(F32) * recency[:, None]
    factor = lax.dynamic_slice_in_dim(factor, first_scene, share, 0)
    factor = jnp.broadcast_to(factor[:, :, None], (share, SIDE, SIDE)).reshape(share, 1, pixels)
    half = jnp.asarray(0.5, BF16)
    width = 2048
    weights = pl.pallas_call(
        cloud_kernel,
        grid=(share, pixels // width),
        in_specs=[in_vmem] * groups
        + [
            pl.BlockSpec((1, 1, width), lambda s, i: (s, 0, i)),
            whole((256, 16)),
            whole((2, 256, 256)),
            whole((8, 256)),
        ],
        out_specs=pl.BlockSpec((1, width // 128, 128), lambda s, i: (s, i, 0)),
        out_shape=jax.ShapeDtypeStruct((share, SIDE // 2, 128), BF16),
        cost_estimate=pl.CostEstimate(flops=12 * 10**9, transcendentals=0, bytes_accessed=10**6),
        name="cloud",
    )(
        *map(keep, layers),
        factor,
        w_in.T * half,
        w_hidden.transpose(0, 2, 1) * half,
        jnp.broadcast_to(w_out[None, :], (8, 256)),
    )
    ids = intersections.reshape(groups, share, 4).transpose(0, 2, 1).reshape(1, scenes * 4)
    ids = jnp.broadcast_to(jnp.pad(ids, ((0, 0), (0, 128 - scenes * 4))).astype(F32), (4, 128))
    all_weights = [weights] + [
        lax.ppermute(weights, "band", [(i, (i + turn) % groups) for i in range(groups)])
        for turn in range(1, groups)
    ]
    theirs = pl.BlockSpec((4, 128, 128), lambda i, b: ((b[0] + 4 - i) % 4, 0, 0))
    moved_weights = pl.pallas_call(
        weight_kernel,
        grid_spec=pltpu.PrefetchScalarGridSpec(
            num_scalar_prefetch=1,
            grid=(groups,),
            in_specs=[whole((share, SIDE // 2, 128))] * groups
            + [whole((4, 128)), theirs, theirs, whole((256, 128)), whole((SIDE, SIDE // 2))],
            out_specs=whole((SIDE, 9, share, 128)),
            scratch_shapes=[pltpu.VMEM((2, SIDE * share, 128), F32)],
        ),
        out_shape=jax.ShapeDtypeStruct((SIDE, 9, share, 128), BF16),
        cost_estimate=pl.CostEstimate(flops=8 * 10**9, transcendentals=0, bytes_accessed=10**6),
        name="reproject_weights",
    )(band.astype(jnp.int32).reshape(1), *all_weights, ids, cols, rows, spread, spread1)
    anywhere = pl.BlockSpec(memory_space=pl.ANY)
    moved_weights = pl.pallas_call(
        after_kernel,
        in_specs=[anywhere, anywhere],
        out_specs=anywhere,
        out_shape=jax.ShapeDtypeStruct(moved_weights.shape, BF16),
        input_output_aliases={0: 0},
        name="after",
    )(moved_weights, keep(values))
    moved_weights = lax.all_to_all(moved_weights, "tile", split_axis=0, concat_axis=0)

    entries = tiles * scenes * 4
    estimate = pl.pallas_call(
        merge_kernel,
        in_specs=[anywhere, in_vmem, in_vmem],
        out_shape=jax.ShapeDtypeStruct((tiles, 4, 128), F32),
        scratch_shapes=[
            pltpu.VMEM((entries, 256), BF16),
            pltpu.VMEM((SIDE, entries), BF16),
            pltpu.VMEM((entries, 128), BF16),
            pltpu.VMEM((tiles, SIDE, 128), F32),
            pltpu.SemaphoreType.DMA,
        ],
        name="merge",
    )(values.reshape(entries, 256), keep(moved_weights), jnp.asarray(double_matrix(), BF16))
    field = lax.all_to_all(estimate, "tile", split_axis=0, concat_axis=0)

    place = jnp.stack([lax.axis_index("tile"), tiles]).astype(jnp.int32)
    out = pl.pallas_call(
        smooth_kernel,
        in_specs=[pl.BlockSpec(memory_space=pltpu.SMEM), in_vmem],
        out_shape=jax.ShapeDtypeStruct((SIDE // 2, 4, 128), F32),
        scratch_shapes=[pltpu.VMEM((4, SIDE, 128), F32)],
        name="smooth",
    )(place, keep(field))
    return out.transpose(1, 0, 2).reshape(4, pixels)


def solution(mesh):
    return jax.shard_map(
        per_device,
        mesh=mesh,
        in_specs=(
            P("tile", "band", None),
            P("tile", None),
            P("tile"),
            P("tile", None),
            P("tile", None, None),
            P("tile", None, None),
            P(),
            P(),
            P(),
        ),
        out_specs=P("band", "tile"),
        check_vma=False,
    )
```

```python
import jax
import jax.numpy as jnp
import numpy as np
from jax import lax
from jax.experimental import pallas as pl
from jax.experimental.pallas import tpu as pltpu
from jax.sharding import PartitionSpec as P

HUBER_ITERS = 4
SMOOTH = 2

prior_weight = 0.25
huber_delta = 0.5
smooth_rate = 0.2

F32 = jnp.float32
BF16 = jnp.bfloat16
SIDE = 64


def dot(a, b, contract=((1,), (0,))):
    return lax.dot_general(a, b, (contract, ((), ())), preferred_element_type=F32)


def spread_matrix(count):
    out = np.zeros((count * SIDE, count * SIDE // 2), np.float32)
    for a in range(count):
        for i in range(SIDE):
            out[a * SIDE + i, count * (i // 2) + a] = 1.0
    return out


def double_matrix():
    eye = huber_delta * np.eye(SIDE, dtype=np.float32)
    return np.kron(np.eye(2, dtype=np.float32), np.concatenate([eye, eye], 1))


def parity_mask(rows):
    row = lax.broadcasted_iota(jnp.int32, (rows, 128), 0)
    lane = lax.broadcasted_iota(jnp.int32, (rows, 128), 1)
    return (row & 1) == (lane >> 6)


def spread_pair(both, mask):
    col = jnp.where(mask, both[:, :128], 0.0).astype(BF16)
    col = col + pltpu.roll(col, 64, 1)
    row = jnp.where(mask, both[:, 128:], 0.0).astype(BF16)
    return col, row


def reproject_kernel(x_ref, col_ref, row_ref, spread_ref, out_ref, scratch):
    mask = parity_mask(256)
    spread = spread_ref[...]
    group = range(8)
    wide = [jnp.concatenate([x_ref[s], col_ref[s], row_ref[s]], 1) for s in group]
    wide = [dot(spread, w) for w in wide]
    planes = [jnp.where(mask, w[:, :128], 0.0).astype(BF16) for w in wide]
    pairs = [spread_pair(w[:, 128:], mask) for w in wide]
    halves = [dot(planes[s], pairs[s][0], ((1,), (1,))).astype(BF16) for s in group]
    for s in group:
        for k in range(4):
            lanes = slice(k * SIDE, (k + 1) * SIDE)
            part = [halves[s][c * SIDE : (c + 1) * SIDE, lanes] for c in range(4)]
            part = jnp.concatenate(part, 1)
            part = jnp.concatenate([part, part], 0)
            moved = dot(pairs[s][1][k * SIDE : (k + 1) * SIDE], part)
            for v in range(2):
                at = pl.ds(4 * k + s % 4, SIDE, stride=16)
                scratch[s // 4, v, at, :] = moved[:, v * 128 : (v + 1) * 128]
    for g in range(2):
        for v in range(2):
            lines = scratch[g, v].reshape(SIDE, 16, 128).astype(BF16)
            out_ref[:, 16 * g : 16 * g + 16, v * 128 : (v + 1) * 128] = lines


def reproject_call(x, cols, rows, name):
    steps = x.shape[0] // 8
    scene_block = pl.BlockSpec((8, 128, 128), lambda i: (i, 0, 0))
    return pl.pallas_call(
        reproject_kernel,
        grid=(steps,),
        in_specs=[scene_block, scene_block, scene_block, whole((256, 128))],
        out_specs=pl.BlockSpec((SIDE, 32, 256), lambda i: (0, i, 0)),
        out_shape=jax.ShapeDtypeStruct((SIDE, 32 * steps, 256), BF16),
        scratch_shapes=[pltpu.VMEM((2, 2, SIDE * 16, 128), F32)],
        name=name,
    )(x, cols, rows, jnp.asarray(spread_matrix(4), BF16))


def weight_kernel(
    band_ref, w0, w1, w2, w3, id_ref, col_ref, row_ref, spread_ref, spread1_ref, out_ref, scratch
):
    turn = pl.program_id(0)
    place = 2 * ((band_ref[0] + 4 - turn) % 4)
    mask = parity_mask(256)
    mask1 = parity_mask(SIDE)
    spread = spread_ref[...]
    spread1 = spread1_ref[...]
    group = range(4)
    w = jnp.where(turn < 2, jnp.where(turn < 1, w0[...], w1[...]), jnp.where(turn < 3, w2[...], w3[...]))
    planes = [jnp.where(mask1, dot(spread1, w[s]), 0.0).astype(BF16) for s in group]
    wide = [dot(spread, jnp.concatenate([col_ref[s], row_ref[s]], 1)) for s in group]
    pairs = [spread_pair(x, mask) for x in wide]
    halves = [dot(planes[s], pairs[s][0], ((1,), (1,))) for s in group]
    for s in group:
        parts = []
        for k in range(4):
            part = halves[s][:, k * SIDE : (k + 1) * SIDE].astype(BF16)
            part = jnp.concatenate([part, part], 0)
            parts.append(dot(pairs[s][1][k * SIDE : (k + 1) * SIDE], part))
        for v in range(2):
            pair = jnp.concatenate(parts[2 * v : 2 * v + 2], 1)
            scratch[v, pl.ds(s, SIDE, stride=4), :] = pair
    for v in range(2):
        out_ref[:, place + v] = scratch[v].reshape(SIDE, 4, 128).astype(BF16)

    @pl.when(turn == 0)
    def _():
        out_ref[:, 8] = jnp.broadcast_to(id_ref[...].astype(BF16)[None], (SIDE, 4, 128))


def after_kernel(x_ref, first_ref, out_ref):
    pass


def cloud_kernel(x0, x1, x2, x3, factor_ref, w_in_ref, w_hidden_ref, w_out_ref, out_ref):
    def silu_of_twice(u):
        return (u + u * jnp.tanh(u)).astype(BF16)

    scene, width = pl.program_id(0), factor_ref.shape[2]
    lanes = pl.ds(pl.multiple_of(pl.program_id(1) * width, width), width)
    x = jnp.concatenate([x_ref[scene, :, lanes] for x_ref in (x0, x1, x2, x3)], 0)
    hidden = silu_of_twice(dot(w_in_ref[...], x))
    for layer in range(2):
        hidden = silu_of_twice(dot(w_hidden_ref[layer], hidden))
    logits = dot(w_out_ref[...], hidden)[:1]
    weight = factor_ref[0] / (1.0 + jnp.exp(logits))
    lines = [weight[:, i * 128 : (i + 1) * 128] for i in range(weight.shape[1] // 128)]
    out_ref[0] = jnp.concatenate(lines, 0).astype(BF16)


def merge_kernel(y_in, w_ref, double_ref, out_ref, y_ref, pick, pick_t, weight, arrival):
    fetch = pltpu.make_async_copy(y_in, y_ref, arrival)
    fetch.start()
    entries = y_ref.shape[0]
    chunk = 1024
    lane = lax.broadcasted_iota(jnp.int32, (1, 128), 1)
    tile = (lax.broadcasted_iota(jnp.int32, (128, 128), 0) & 63).astype(F32).astype(BF16)
    one, none = jnp.ones((128, 128), BF16), jnp.zeros((128, 128), BF16)
    ids = w_ref[:, 8].astype(F32)[:, 0, :]
    turned = pltpu.roll(ids, 64, 1)
    for i in range(entries // 128):
        span = slice(i * 128, (i + 1) * 128)
        pair = jnp.where(lane < 64, ids[2 * i : 2 * i + 1], turned[2 * i + 1 : 2 * i + 2])
        hit = jnp.where(jnp.broadcast_to(pair, (128, 128)).astype(BF16) == tile, one, none)
        pick[:, span] = hit[:SIDE]
        pick_t[span, :] = hit.T
    for i in range(8):
        w = dot(w_ref[:, i].reshape(entries // 16, 128), double_ref[...])
        for half in range(2):
            first = 8 * i + 4 * half
            weight[:, first : first + 4, :] = w[:, half * 128 : (half + 1) * 128].reshape(
                entries // SIDE, 4, 128
            )
    fetch.wait()

    def totals(estimate):
        top = bottom = 0.0
        if estimate is not None:
            high = estimate.astype(BF16)
            low = (estimate - high.astype(F32)).astype(BF16)
            stacked = jnp.concatenate([high, low], 0)
        spans = [slice(i * chunk, (i + 1) * chunk) for i in range(entries // chunk)]

        def expected(span):
            return None if estimate is None else dot(pick_t[span, :], stacked)

        ahead = expected(spans[0])
        for i, span in enumerate(spans):
            here, ahead = ahead, expected(spans[i + 1]) if i + 1 < len(spans) else None
            w = weight[i * chunk // SIDE : (i + 1) * chunk // SIDE].reshape(chunk, 128)
            y = y_ref[span, :]
            h = jnp.concatenate([w, w], 1)
            if estimate is not None:
                h = h / jnp.maximum(jnp.abs(y.astype(F32) - here), huber_delta)
            h = h.astype(BF16)
            picked = pick[:, span]
            top = top + dot(picked, h * y)
            bottom = bottom + dot(picked, h[:, :128] if estimate is None else h)
        if estimate is None:
            bottom = jnp.concatenate([bottom, bottom], 1)
        prior = prior_weight if estimate is not None else prior_weight * huber_delta
        return top / (bottom + prior)

    estimate = lax.fori_loop(0, HUBER_ITERS, lambda _, e: totals(e), totals(None))

    lane = lax.broadcasted_iota(jnp.int32, (SIDE, 128), 1)
    for v in range(2):
        own = estimate[:, v * 128 : (v + 1) * 128]
        turned = pltpu.roll(own, 64, 1)
        for odd in range(2):
            first, second = (turned, own) if odd else (own, turned)
            after = pltpu.roll(second, SIDE - 1, 0)
            before = pltpu.roll(second, 1, 0)
            out_ref[:, 2 * v + odd, :] = jnp.where(
                lane < 64, first, jnp.where(lane < 96, after, before)
            )


def smooth_kernel(tile_ref, g_ref, out_ref, scratch):
    first = tile_ref[0] == 0
    last = tile_ref[0] == tile_ref[1] - 1
    lane = lax.broadcasted_iota(jnp.int32, (SIDE, 128), 1)
    row = lax.broadcasted_iota(jnp.int32, (SIDE, 128), 0)
    closed = ((lane == 127) & first) | ((lane == SIDE - 1) & last)
    bottom = row == SIDE - 1

    def flux(d):
        return d / (1.0 + d * d)

    for c in range(4):
        g = g_ref[:, c, :]
        for repeat in range(SMOOTH):
            across = jnp.where(closed, 0.0, flux(pltpu.roll(g, 127, 1) - g))
            down = jnp.where(bottom, 0.0, flux(pltpu.roll(g, SIDE - 1, 0) - g))
            g = g + smooth_rate * (
                across - pltpu.roll(across, 1, 1) + (down - pltpu.roll(down, 1, 0))
            )
        scratch[c] = g
        even = scratch[c, pl.ds(0, SIDE // 2, stride=2), :]
        odd = scratch[c, pl.ds(1, SIDE // 2, stride=2), :]
        out_ref[:, c, :] = jnp.where(lane[: SIDE // 2] < SIDE, even, pltpu.roll(odd, SIDE, 1))


def two_rows_per_line(x):
    scenes, planes, _ = x.shape
    x = x.reshape(scenes, planes, SIDE // 2, 128)
    return x.transpose(0, 2, 1, 3).reshape(scenes, planes * SIDE // 2, 128)


def keep(x):
    return pltpu.with_memory_space_constraint(x, pltpu.VMEM)


def whole(shape):
    return pl.BlockSpec(shape, lambda *_: (0,) * len(shape))


def per_device(
    granules,
    valid_rows,
    scene_order,
    intersections,
    row_resample,
    col_resample,
    w_in,
    w_hidden,
    w_out,
):
    scenes, bands, pixels = granules.shape
    tiles = lax.axis_size("tile")
    groups = lax.axis_size("band")
    share = scenes // groups
    spread = jnp.asarray(spread_matrix(4), BF16)
    spread1 = jnp.asarray(spread_matrix(1), BF16)

    in_vmem = pl.BlockSpec(memory_space=pltpu.VMEM)
    cols = two_rows_per_line(col_resample)
    rows = two_rows_per_line(row_resample)
    moved = reproject_call(two_rows_per_line(granules), cols, rows, "reproject")
    moved, granules = lax.optimization_barrier((moved, granules))
    values = lax.all_to_all(moved, "tile", split_axis=0, concat_axis=0)

    band = lax.axis_index("band")
    by_group = granules.reshape(groups, share, bands, pixels)
    w_in = w_in.reshape(groups, bands, -1)
    layers, w_rows = [], []
    for turn in range(groups):
        part = lax.dynamic_index_in_dim(by_group, (band + turn) % groups, 0, keepdims=False)
        if turn:
            part = lax.ppermute(part, "band", [(i, (i + turn) % groups) for i in range(groups)])
        layers.append(part)
        w_rows.append(lax.dynamic_index_in_dim(w_in, (band - turn) % groups, 0, keepdims=False))
    w_in = jnp.concatenate(w_rows, 0)

    first_scene = band * share
    recency = jnp.exp(1.4 * scene_order.astype(F32) / (scenes * tiles) - 0.7)
    factor = valid_rows.astype(F32) * recency[:, None]
    factor = lax.dynamic_slice_in_dim(factor, first_scene, share, 0)
    factor = jnp.broadcast_to(factor[:, :, None], (share, SIDE, SIDE)).reshape(share, 1, pixels)
    half = jnp.asarray(0.5, BF16)
    width = 2048
    weights = pl.pallas_call(
        cloud_kernel,
        grid=(share, pixels // width),
        in_specs=[in_vmem] * groups
        + [
            pl.BlockSpec((1, 1, width), lambda s, i: (s, 0, i)),
            whole((256, 16)),
            whole((2, 256, 256)),
            whole((8, 256)),
        ],
        out_specs=pl.BlockSpec((1, width // 128, 128), lambda s, i: (s, i, 0)),
        out_shape=jax.ShapeDtypeStruct((share, SIDE // 2, 128), BF16),
        cost_estimate=pl.CostEstimate(flops=12 * 10**9, transcendentals=0, bytes_accessed=10**6),
        name="cloud",
    )(
        *map(keep, layers),
        factor,
        w_in.T * half,
        w_hidden.transpose(0, 2, 1) * half,
        jnp.broadcast_to(w_out[None, :], (8, 256)),
    )
    ids = intersections.reshape(groups, share, 4).transpose(0, 2, 1).reshape(1, scenes * 4)
    ids = jnp.broadcast_to(jnp.pad(ids, ((0, 0), (0, 128 - scenes * 4))).astype(F32), (4, 128))
    all_weights = [weights] + [
        lax.ppermute(weights, "band", [(i, (i + turn) % groups) for i in range(groups)])
        for turn in range(1, groups)
    ]
    theirs = pl.BlockSpec((4, 128, 128), lambda i, b: ((b[0] + 4 - i) % 4, 0, 0))
    moved_weights = pl.pallas_call(
        weight_kernel,
        grid_spec=pltpu.PrefetchScalarGridSpec(
            num_scalar_prefetch=1,
            grid=(groups,),
            in_specs=[whole((share, SIDE // 2, 128))] * groups
            + [whole((4, 128)), theirs, theirs, whole((256, 128)), whole((SIDE, SIDE // 2))],
            out_specs=whole((SIDE, 9, share, 128)),
            scratch_shapes=[pltpu.VMEM((2, SIDE * share, 128), F32)],
        ),
        out_shape=jax.ShapeDtypeStruct((SIDE, 9, share, 128), BF16),
        cost_estimate=pl.CostEstimate(flops=8 * 10**9, transcendentals=0, bytes_accessed=10**6),
        name="reproject_weights",
    )(band.astype(jnp.int32).reshape(1), *all_weights, ids, cols, rows, spread, spread1)
    anywhere = pl.BlockSpec(memory_space=pl.ANY)
    moved_weights = pl.pallas_call(
        after_kernel,
        in_specs=[anywhere, anywhere],
        out_specs=anywhere,
        out_shape=jax.ShapeDtypeStruct(moved_weights.shape, BF16),
        input_output_aliases={0: 0},
        name="after",
    )(moved_weights, keep(values))
    moved_weights = lax.all_to_all(moved_weights, "tile", split_axis=0, concat_axis=0)

    entries = tiles * scenes * 4
    estimate = pl.pallas_call(
        merge_kernel,
        in_specs=[anywhere, in_vmem, in_vmem],
        out_shape=jax.ShapeDtypeStruct((tiles, 4, 128), F32),
        scratch_shapes=[
            pltpu.VMEM((entries, 256), BF16),
            pltpu.VMEM((SIDE, entries), BF16),
            pltpu.VMEM((entries, 128), BF16),
            pltpu.VMEM((tiles, SIDE, 128), F32),
            pltpu.SemaphoreType.DMA,
        ],
        name="merge",
    )(values.reshape(entries, 256), keep(moved_weights), jnp.asarray(double_matrix(), BF16))
    field = lax.all_to_all(estimate, "tile", split_axis=0, concat_axis=0)

    place = jnp.stack([lax.axis_index("tile"), tiles]).astype(jnp.int32)
    out = pl.pallas_call(
        smooth_kernel,
        in_specs=[pl.BlockSpec(memory_space=pltpu.SMEM), in_vmem],
        out_shape=jax.ShapeDtypeStruct((SIDE // 2, 4, 128), F32),
        scratch_shapes=[pltpu.VMEM((4, SIDE, 128), F32)],
        name="smooth",
    )(place, keep(field))
    return out.transpose(1, 0, 2).reshape(4, pixels)


def solution(mesh):
    return jax.shard_map(
        per_device,
        mesh=mesh,
        in_specs=(
            P("tile", "band", None),
            P("tile", None),
            P("tile"),
            P("tile", None),
            P("tile", None, None),
            P("tile", None, None),
            P(),
            P(),
            P(),
        ),
        out_specs=P("band", "tile"),
        check_vma=False,
    )
```

```python
import jax
import jax.numpy as jnp
import numpy as np
from jax import lax
from jax.experimental import pallas as pl
from jax.experimental.pallas import tpu as pltpu
from jax.sharding import PartitionSpec as P

HUBER_ITERS = 4
SMOOTH = 2

prior_weight = 0.25
huber_delta = 0.5
smooth_rate = 0.2

F32 = jnp.float32
BF16 = jnp.bfloat16
SIDE = 64


def dot(a, b, contract=((1,), (0,))):
    return lax.dot_general(a, b, (contract, ((), ())), preferred_element_type=F32)


def spread_matrix(count):
    out = np.zeros((count * SIDE, count * SIDE // 2), np.float32)
    for a in range(count):
        for i in range(SIDE):
            out[a * SIDE + i, count * (i // 2) + a] = 1.0
    return out


def double_matrix():
    eye = huber_delta * np.eye(SIDE, dtype=np.float32)
    return np.kron(np.eye(2, dtype=np.float32), np.concatenate([eye, eye], 1))


def parity_mask(rows):
    row = lax.broadcasted_iota(jnp.int32, (rows, 128), 0)
    lane = lax.broadcasted_iota(jnp.int32, (rows, 128), 1)
    return (row & 1) == (lane >> 6)


def spread_pair(both, mask):
    col = jnp.where(mask, both[:, :128], 0.0).astype(BF16)
    col = col + pltpu.roll(col, 64, 1)
    row = jnp.where(mask, both[:, 128:], 0.0).astype(BF16)
    return col, row


def reproject_kernel(x_ref, col_ref, row_ref, spread_ref, out_ref, scratch):
    mask = parity_mask(256)
    spread = spread_ref[...]
    group = range(8)
    wide = [jnp.concatenate([x_ref[s], col_ref[s], row_ref[s]], 1) for s in group]
    wide = [dot(spread, w) for w in wide]
    planes = [jnp.where(mask, w[:, :128], 0.0).astype(BF16) for w in wide]
    pairs = [spread_pair(w[:, 128:], mask) for w in wide]
    halves = [dot(planes[s], pairs[s][0], ((1,), (1,))).astype(BF16) for s in group]
    for s in group:
        for k in range(4):
            lanes = slice(k * SIDE, (k + 1) * SIDE)
            part = [halves[s][c * SIDE : (c + 1) * SIDE, lanes] for c in range(4)]
            part = jnp.concatenate(part, 1)
            part = jnp.concatenate([part, part], 0)
            moved = dot(pairs[s][1][k * SIDE : (k + 1) * SIDE], part)
            for v in range(2):
                at = pl.ds(4 * k + s % 4, SIDE, stride=16)
                scratch[s // 4, v, at, :] = moved[:, v * 128 : (v + 1) * 128]
    for g in range(2):
        for v in range(2):
            lines = scratch[g, v].reshape(SIDE, 16, 128).astype(BF16)
            out_ref[:, 16 * g : 16 * g + 16, v * 128 : (v + 1) * 128] = lines


def reproject_call(x, cols, rows, name):
    steps = x.shape[0] // 8
    scene_block = pl.BlockSpec((8, 128, 128), lambda i: (i, 0, 0))
    return pl.pallas_call(
        reproject_kernel,
        grid=(steps,),
        in_specs=[scene_block, scene_block, scene_block, whole((256, 128))],
        out_specs=pl.BlockSpec((SIDE, 32, 256), lambda i: (0, i, 0)),
        out_shape=jax.ShapeDtypeStruct((SIDE, 32 * steps, 256), BF16),
        scratch_shapes=[pltpu.VMEM((2, 2, SIDE * 16, 128), F32)],
        name=name,
    )(x, cols, rows, jnp.asarray(spread_matrix(4), BF16))


def weight_kernel(
    band_ref, w0, w1, w2, w3, id_ref, col_ref, row_ref, spread_ref, spread1_ref, out_ref, scratch
):
    turn = pl.program_id(0)
    place = 2 * ((band_ref[0] + 4 - turn) % 4)
    mask = parity_mask(256)
    mask1 = parity_mask(SIDE)
    spread = spread_ref[...]
    spread1 = spread1_ref[...]
    group = range(4)
    w = jnp.where(turn < 2, jnp.where(turn < 1, w0[...], w1[...]), jnp.where(turn < 3, w2[...], w3[...]))
    planes = [jnp.where(mask1, dot(spread1, w[s]), 0.0).astype(BF16) for s in group]
    wide = [dot(spread, jnp.concatenate([col_ref[s], row_ref[s]], 1)) for s in group]
    pairs = [spread_pair(x, mask) for x in wide]
    halves = [dot(planes[s], pairs[s][0], ((1,), (1,))) for s in group]
    for s in group:
        parts = []
        for k in range(4):
            part = halves[s][:, k * SIDE : (k + 1) * SIDE].astype(BF16)
            part = jnp.concatenate([part, part], 0)
            parts.append(dot(pairs[s][1][k * SIDE : (k + 1) * SIDE], part))
        for v in range(2):
            pair = jnp.concatenate(parts[2 * v : 2 * v + 2], 1)
            scratch[v, pl.ds(s, SIDE, stride=4), :] = pair
    for v in range(2):
        out_ref[:, place + v] = scratch[v].reshape(SIDE, 4, 128).astype(BF16)

    @pl.when(turn == 0)
    def _():
        out_ref[:, 8] = jnp.broadcast_to(id_ref[...].astype(BF16)[None], (SIDE, 4, 128))


def after_kernel(x_ref, first_ref, out_ref):
    pass


def cloud_kernel(x0, x1, x2, x3, factor_ref, w_in_ref, w_hidden_ref, w_out_ref, out_ref):
    def silu_of_twice(u):
        return (u + u * jnp.tanh(u)).astype(BF16)

    scene, width = pl.program_id(0), factor_ref.shape[2]
    lanes = pl.ds(pl.multiple_of(pl.program_id(1) * width, width), width)
    x = jnp.concatenate([x_ref[scene, :, lanes] for x_ref in (x0, x1, x2, x3)], 0)
    hidden = silu_of_twice(dot(w_in_ref[...], x))
    for layer in range(2):
        hidden = silu_of_twice(dot(w_hidden_ref[layer], hidden))
    logits = dot(w_out_ref[...], hidden)[:1]
    weight = factor_ref[0] / (1.0 + jnp.exp(logits))
    lines = [weight[:, i * 128 : (i + 1) * 128] for i in range(weight.shape[1] // 128)]
    out_ref[0] = jnp.concatenate(lines, 0).astype(BF16)


def merge_kernel(y_in, w_ref, double_ref, out_ref, y_ref, pick, pick_t, weight, arrival):
    fetch = pltpu.make_async_copy(y_in, y_ref, arrival)
    fetch.start()
    entries = y_ref.shape[0]
    chunk = 1024
    lane = lax.broadcasted_iota(jnp.int32, (1, 128), 1)
    tile = (lax.broadcasted_iota(jnp.int32, (128, 128), 0) & 63).astype(F32)
    ids = w_ref[:, 8].astype(F32)[:, 0, :]
    turned = pltpu.roll(ids, 64, 1)
    for i in range(entries // 128):
        span = slice(i * 128, (i + 1) * 128)
        pair = jnp.where(lane < 64, ids[2 * i : 2 * i + 1], turned[2 * i + 1 : 2 * i + 2])
        hit = jnp.where(pair == tile, 1.0, 0.0)
        pick[:, span] = hit[:SIDE].astype(BF16)
        pick_t[span, :] = hit.T.astype(BF16)
    for i in range(8):
        w = dot(w_ref[:, i].reshape(entries // 16, 128), double_ref[...])
        for half in range(2):
            first = 8 * i + 4 * half
            weight[:, first : first + 4, :] = w[:, half * 128 : (half + 1) * 128].reshape(
                entries // SIDE, 4, 128
            )
    fetch.wait()

    def totals(estimate):
        top = bottom = 0.0
        if estimate is not None:
            high = estimate.astype(BF16)
            low = (estimate - high.astype(F32)).astype(BF16)
            stacked = jnp.concatenate([high, low], 0)
        spans = [slice(i * chunk, (i + 1) * chunk) for i in range(entries // chunk)]

        def expected(span):
            return None if estimate is None else dot(pick_t[span, :], stacked)

        ahead = expected(spans[0])
        for i, span in enumerate(spans):
            here, ahead = ahead, expected(spans[i + 1]) if i + 1 < len(spans) else None
            w = weight[i * chunk // SIDE : (i + 1) * chunk // SIDE].reshape(chunk, 128)
            y = y_ref[span, :]
            h = jnp.concatenate([w, w], 1)
            if estimate is not None:
                h = h / jnp.maximum(jnp.abs(y.astype(F32) - here), huber_delta)
            h = h.astype(BF16)
            picked = pick[:, span]
            top = top + dot(picked, h * y)
            bottom = bottom + dot(picked, h)
        prior = prior_weight if estimate is not None else prior_weight * huber_delta
        return top / (bottom + prior)

    estimate = lax.fori_loop(0, HUBER_ITERS, lambda _, e: totals(e), totals(None))

    lane = lax.broadcasted_iota(jnp.int32, (SIDE, 128), 1)
    for v in range(2):
        own = estimate[:, v * 128 : (v + 1) * 128]
        turned = pltpu.roll(own, 64, 1)
        for odd in range(2):
            first, second = (turned, own) if odd else (own, turned)
            after = pltpu.roll(second, SIDE - 1, 0)
            before = pltpu.roll(second, 1, 0)
            out_ref[:, 2 * v + odd, :] = jnp.where(
                lane < 64, first, jnp.where(lane < 96, after, before)
            )


def smooth_kernel(tile_ref, g_ref, out_ref, scratch):
    first = tile_ref[0] == 0
    last = tile_ref[0] == tile_ref[1] - 1
    lane = lax.broadcasted_iota(jnp.int32, (SIDE, 128), 1)
    row = lax.broadcasted_iota(jnp.int32, (SIDE, 128), 0)
    closed = ((lane == 127) & first) | ((lane == SIDE - 1) & last)
    bottom = row == SIDE - 1

    def flux(d):
        return d / (1.0 + d * d)

    bands = [g_ref[:, c, :] for c in range(4)]
    for repeat in range(SMOOTH):
        across = [jnp.where(closed, 0.0, flux(pltpu.roll(g, 127, 1) - g)) for g in bands]
        down = [jnp.where(bottom, 0.0, flux(pltpu.roll(g, SIDE - 1, 0) - g)) for g in bands]
        across = [a - pltpu.roll(a, 1, 1) for a in across]
        down = [d - pltpu.roll(d, 1, 0) for d in down]
        bands = [g + smooth_rate * (a + d) for g, a, d in zip(bands, across, down)]
    for c in range(4):
        scratch[c] = bands[c]
    for c in range(4):
        even = scratch[c, pl.ds(0, SIDE // 2, stride=2), :]
        odd = scratch[c, pl.ds(1, SIDE // 2, stride=2), :]
        out_ref[:, c, :] = jnp.where(lane[: SIDE // 2] < SIDE, even, pltpu.roll(odd, SIDE, 1))


def two_rows_per_line(x):
    scenes, planes, _ = x.shape
    x = x.reshape(scenes, planes, SIDE // 2, 128)
    return x.transpose(0, 2, 1, 3).reshape(scenes, planes * SIDE // 2, 128)


def keep(x):
    return pltpu.with_memory_space_constraint(x, pltpu.VMEM)


def whole(shape):
    return pl.BlockSpec(shape, lambda *_: (0,) * len(shape))


def per_device(
    granules,
    valid_rows,
    scene_order,
    intersections,
    row_resample,
    col_resample,
    w_in,
    w_hidden,
    w_out,
):
    scenes, bands, pixels = granules.shape
    tiles = lax.axis_size("tile")
    groups = lax.axis_size("band")
    share = scenes // groups
    spread = jnp.asarray(spread_matrix(4), BF16)
    spread1 = jnp.asarray(spread_matrix(1), BF16)

    in_vmem = pl.BlockSpec(memory_space=pltpu.VMEM)
    cols = two_rows_per_line(col_resample)
    rows = two_rows_per_line(row_resample)
    moved = reproject_call(two_rows_per_line(granules), cols, rows, "reproject")
    moved, granules = lax.optimization_barrier((moved, granules))
    values = lax.all_to_all(moved, "tile", split_axis=0, concat_axis=0)

    band = lax.axis_index("band")
    by_group = granules.reshape(groups, share, bands, pixels)
    w_in = w_in.reshape(groups, bands, -1)
    layers, w_rows = [], []
    for turn in range(groups):
        part = lax.dynamic_index_in_dim(by_group, (band + turn) % groups, 0, keepdims=False)
        if turn:
            part = lax.ppermute(part, "band", [(i, (i + turn) % groups) for i in range(groups)])
        layers.append(part)
        w_rows.append(lax.dynamic_index_in_dim(w_in, (band - turn) % groups, 0, keepdims=False))
    w_in = jnp.concatenate(w_rows, 0)

    first_scene = band * share
    recency = jnp.exp(1.4 * scene_order.astype(F32) / (scenes * tiles) - 0.7)
    factor = valid_rows.astype(F32) * recency[:, None]
    factor = lax.dynamic_slice_in_dim(factor, first_scene, share, 0)
    factor = jnp.broadcast_to(factor[:, :, None], (share, SIDE, SIDE)).reshape(share, 1, pixels)
    half = jnp.asarray(0.5, BF16)
    width = 2048
    weights = pl.pallas_call(
        cloud_kernel,
        grid=(share, pixels // width),
        in_specs=[in_vmem] * groups
        + [
            pl.BlockSpec((1, 1, width), lambda s, i: (s, 0, i)),
            whole((256, 16)),
            whole((2, 256, 256)),
            whole((8, 256)),
        ],
        out_specs=pl.BlockSpec((1, width // 128, 128), lambda s, i: (s, i, 0)),
        out_shape=jax.ShapeDtypeStruct((share, SIDE // 2, 128), BF16),
        cost_estimate=pl.CostEstimate(flops=12 * 10**9, transcendentals=0, bytes_accessed=10**6),
        name="cloud",
    )(
        *map(keep, layers),
        factor,
        w_in.T * half,
        w_hidden.transpose(0, 2, 1) * half,
        jnp.broadcast_to(w_out[None, :], (8, 256)),
    )
    ids = intersections.reshape(groups, share, 4).transpose(0, 2, 1).reshape(1, scenes * 4)
    ids = jnp.broadcast_to(jnp.pad(ids, ((0, 0), (0, 128 - scenes * 4))).astype(F32), (4, 128))
    all_weights = [weights] + [
        lax.ppermute(weights, "band", [(i, (i + turn) % groups) for i in range(groups)])
        for turn in range(1, groups)
    ]
    theirs = pl.BlockSpec((4, 128, 128), lambda i, b: ((b[0] + 4 - i) % 4, 0, 0))
    moved_weights = pl.pallas_call(
        weight_kernel,
        grid_spec=pltpu.PrefetchScalarGridSpec(
            num_scalar_prefetch=1,
            grid=(groups,),
            in_specs=[whole((share, SIDE // 2, 128))] * groups
            + [whole((4, 128)), theirs, theirs, whole((256, 128)), whole((SIDE, SIDE // 2))],
            out_specs=whole((SIDE, 9, share, 128)),
            scratch_shapes=[pltpu.VMEM((2, SIDE * share, 128), F32)],
        ),
        out_shape=jax.ShapeDtypeStruct((SIDE, 9, share, 128), BF16),
        cost_estimate=pl.CostEstimate(flops=8 * 10**9, transcendentals=0, bytes_accessed=10**6),
        name="reproject_weights",
    )(band.astype(jnp.int32).reshape(1), *all_weights, ids, cols, rows, spread, spread1)
    anywhere = pl.BlockSpec(memory_space=pl.ANY)
    moved_weights = pl.pallas_call(
        after_kernel,
        in_specs=[anywhere, anywhere],
        out_specs=anywhere,
        out_shape=jax.ShapeDtypeStruct(moved_weights.shape, BF16),
        input_output_aliases={0: 0},
        name="after",
    )(moved_weights, keep(values))
    moved_weights = lax.all_to_all(moved_weights, "tile", split_axis=0, concat_axis=0)

    entries = tiles * scenes * 4
    estimate = pl.pallas_call(
        merge_kernel,
        in_specs=[anywhere, in_vmem, in_vmem],
        out_shape=jax.ShapeDtypeStruct((tiles, 4, 128), F32),
        scratch_shapes=[
            pltpu.VMEM((entries, 256), BF16),
            pltpu.VMEM((SIDE, entries), BF16),
            pltpu.VMEM((entries, 128), BF16),
            pltpu.VMEM((tiles, SIDE, 128), F32),
            pltpu.SemaphoreType.DMA,
        ],
        name="merge",
    )(values.reshape(entries, 256), keep(moved_weights), jnp.asarray(double_matrix(), BF16))
    field = lax.all_to_all(estimate, "tile", split_axis=0, concat_axis=0)

    place = jnp.stack([lax.axis_index("tile"), tiles]).astype(jnp.int32)
    out = pl.pallas_call(
        smooth_kernel,
        in_specs=[pl.BlockSpec(memory_space=pltpu.SMEM), in_vmem],
        out_shape=jax.ShapeDtypeStruct((SIDE // 2, 4, 128), F32),
        scratch_shapes=[pltpu.VMEM((4, SIDE, 128), F32)],
        name="smooth",
    )(place, keep(field))
    return out.transpose(1, 0, 2).reshape(4, pixels)


def solution(mesh):
    return jax.shard_map(
        per_device,
        mesh=mesh,
        in_specs=(
            P("tile", "band", None),
            P("tile", None),
            P("tile"),
            P("tile", None),
            P("tile", None, None),
            P("tile", None, None),
            P(),
            P(),
            P(),
        ),
        out_specs=P("band", "tile"),
        check_vma=False,
    )
```
